256 devices in a mesh: ctx: 128 (over y, x_lo, z, core), head: 2 (over x_hi).
Axes of the slice: x: 4 (x_hi: 2, x_lo: 2; x = x_hi * 2 + x_lo), y: 4, z: 8, core: 2. Of those that a mesh axis runs over, the one named last changes fastest.
Arguments:
- queries: bfloat16 [8192, 2048], P('ctx', 'head'), may hold values from -6 to 6
- keys_first: bfloat16 [8192, 512], P('ctx', 'head'), may hold values from -6 to 6
- primary_value_array: bfloat16 [8192, 512], P('ctx', 'head'), may hold values from -6 to 6
- keys_second: bfloat16 [8192, 512], P('ctx', 'head'), may hold values from -6 to 6
- secondary_value_array: bfloat16 [8192, 512], P('ctx', 'head'), may hold values from -6 to 6
- out_weight: bfloat16 [2048, 4096], P('head'), may hold values from -6 to 6
Outputs:
- projected: bfloat16 [8192, 4096], P('ctx', 'head')
The draws below stay inside these ranges and needn't reach their ends.
All inputs are finite; a program needn't handle non-finite values.
Results may differ from the reference program's by a relative error of at most 0.01.
Values may be sent and summed in bfloat16 or wider, within the bound.
No kernel may reach another device: no remote copies, remote signals or barrier semaphores. Data moves between devices by JAX's collectives and lax.ppermute only.
A program may use at most 128 MiB of HBM per device.

```python
import math
import jax
import jax.numpy as jnp
from jax import lax

D = 4096
QUERY_HEADS = 16
KEY_VALUE_HEADS = 4
HEAD_SIZE = 128
FIRST_WINDOW = 512
SECOND_WINDOW = 16
TOKENS_PER_SHARE = 64
TOKEN_COUNT = 8192


def draw_queries(key, part):
    final_output = jax.random.truncated_normal(jax.random.fold_in(key, 11), -6.0, 6.0, (TOKEN_COUNT, QUERY_HEADS * HEAD_SIZE), jnp.float32)
    return final_output.astype(jnp.bfloat16)


def draw_keys_first(key, part):
    final_output = jax.random.truncated_normal(jax.random.fold_in(key, 12), -6.0, 6.0, (TOKEN_COUNT, KEY_VALUE_HEADS * HEAD_SIZE), jnp.float32)
    return final_output.astype(jnp.bfloat16)


def draw_keys_second(key, part):
    final_output = jax.random.truncated_normal(jax.random.fold_in(key, 13), -6.0, 6.0, (TOKEN_COUNT, KEY_VALUE_HEADS * HEAD_SIZE), jnp.float32)
    return final_output.astype(jnp.bfloat16)


def shard_levels(own_key, extent, split, low, top_value):
    level, own = 1.0, jax.random.fold_in(own_key, 6)
    for position, blocks in split:
        steps = jnp.exp(jax.random.uniform(jax.random.fold_in(own, position), (blocks,), jnp.float32, low / len(split), top_value / len(split)))
        level = level * jnp.repeat(steps, extent[position] // blocks).reshape([-1 if axis == position else 1 for axis in range(len(extent))])
    return level


def centred(own_key, shape, width, most, pieces=(), kind=jnp.bfloat16):
    values = jax.random.normal(own_key, shape, jnp.float32) * width
    if len(pieces) > 0:
        values = shard_levels(own_key, shape, pieces, -0.22, 0.18) * values
    return jnp.clip(values, min=-most, max=most).astype(kind)


def setup_inputs(seed: int = 0) -> dict:
    arg_keys = jax.random.split(jax.random.key(seed), 7)
    return {
        "queries": draw_queries(jax.random.fold_in(arg_keys[6], 71), 0),
        "keys_first": draw_keys_first(jax.random.fold_in(arg_keys[6], 71), 0),
        "primary_value_array": centred(arg_keys[2], (TOKEN_COUNT, KEY_VALUE_HEADS * HEAD_SIZE), 1.0, 6.0, ((0, 128), (1, 2))),
        "keys_second": draw_keys_second(jax.random.fold_in(arg_keys[6], 71), 0),
        "secondary_value_array": centred(arg_keys[4], (TOKEN_COUNT, KEY_VALUE_HEADS * HEAD_SIZE), 1.0, 6.0, ((0, 128), (1, 2))),
        "out_weight": centred(arg_keys[5], (QUERY_HEADS * HEAD_SIZE, D), 1.0, 6.0, ((0, 2),)),
    }


NEGATIVE = -1e+30

def reference(queries, keys_first, primary_value_array, keys_second, secondary_value_array, out_weight):
    group_count = QUERY_HEADS // KEY_VALUE_HEADS
    score_scale = 1.0 / math.sqrt(HEAD_SIZE)
    column_span = KEY_VALUE_HEADS * HEAD_SIZE
    padded_keys = jnp.concatenate([jnp.zeros((FIRST_WINDOW, column_span), keys_first.dtype), keys_first], axis=0)
    padded_values = jnp.concatenate([jnp.zeros((FIRST_WINDOW, column_span), primary_value_array.dtype), primary_value_array], axis=0)
    padded_second = jnp.concatenate([jnp.zeros((SECOND_WINDOW, column_span), keys_second.dtype), keys_second], axis=0)
    padded_svalues = jnp.concatenate([jnp.zeros((SECOND_WINDOW, column_span), secondary_value_array.dtype), secondary_value_array], axis=0)

    def one_block(block_index):
        block_start = (block_index * TOKENS_PER_SHARE).astype(jnp.int32)
        rows_of_query = lax.dynamic_slice_in_dim(queries, block_start, TOKENS_PER_SHARE, 0)
        primary_keys = lax.dynamic_slice_in_dim(padded_keys, block_start, FIRST_WINDOW + TOKENS_PER_SHARE, 0)
        primary_values = lax.dynamic_slice_in_dim(padded_values, block_start, FIRST_WINDOW + TOKENS_PER_SHARE, 0)
        second_slab = lax.dynamic_slice_in_dim(padded_second, block_start + 1, TOKENS_PER_SHARE + SECOND_WINDOW - 1, 0)
        svalue_slab = lax.dynamic_slice_in_dim(padded_svalues, block_start + 1, TOKENS_PER_SHARE + SECOND_WINDOW - 1, 0)
        secondary_keys = jnp.stack([second_slab[offset:offset + TOKENS_PER_SHARE] for offset in range(SECOND_WINDOW)], axis=1)
        secondary_values = jnp.stack([svalue_slab[offset:offset + TOKENS_PER_SHARE] for offset in range(SECOND_WINDOW)], axis=1)
        head_queries = rows_of_query.astype(jnp.float32).reshape(TOKENS_PER_SHARE, KEY_VALUE_HEADS, group_count, HEAD_SIZE).transpose(1, 2, 0, 3)[:, :, :, None, :]
        secondary_heads = secondary_keys.astype(jnp.float32).reshape(TOKENS_PER_SHARE, SECOND_WINDOW, KEY_VALUE_HEADS, HEAD_SIZE).transpose(2, 0, 1, 3)[:, None]
        secondary_value_heads = secondary_values.astype(jnp.float32).reshape(TOKENS_PER_SHARE, SECOND_WINDOW, KEY_VALUE_HEADS, HEAD_SIZE).transpose(2, 0, 1, 3)[:, None]
        products = (head_queries * secondary_heads * score_scale).astype(jnp.bfloat16)
        products = lax.optimization_barrier(products).astype(jnp.float32)
        head_keys = primary_keys.astype(jnp.float32).reshape(FIRST_WINDOW + TOKENS_PER_SHARE, KEY_VALUE_HEADS, HEAD_SIZE)
        head_values = primary_values.astype(jnp.float32).reshape(FIRST_WINDOW + TOKENS_PER_SHARE, KEY_VALUE_HEADS, HEAD_SIZE)
        scores = jnp.einsum('gmtod,jgd->gmjto', products, head_keys, precision=lax.Precision.HIGHEST)
        key_pos = block_start - FIRST_WINDOW + jnp.arange(FIRST_WINDOW + TOKENS_PER_SHARE, dtype=jnp.int32)
        query_pos = block_start + jnp.arange(TOKENS_PER_SHARE, dtype=jnp.int32)
        second_pos = query_pos[:, None] - SECOND_WINDOW + 1 + jnp.arange(SECOND_WINDOW, dtype=jnp.int32)[None, :]
        allowed_pairs = (key_pos[:, None] <= query_pos[None, :]) & (key_pos[:, None] > query_pos[None, :] - FIRST_WINDOW) & (key_pos[:, None] >= 0)
        allowed_pairs = allowed_pairs[:, :, None] & (second_pos >= 0)[None]
        masked = jnp.where(allowed_pairs, scores, NEGATIVE)
        row_top = lax.optimization_barrier(jnp.max(masked, axis=(2, 4), keepdims=True))
        expo = jnp.where(allowed_pairs, jnp.exp(scores - row_top), 0.0)
        row_total = lax.optimization_barrier(jnp.sum(expo, axis=(2, 4)))
        weights = lax.optimization_barrier(expo.astype(jnp.bfloat16)).astype(jnp.float32)
        mixture = jnp.einsum('gmjto,jgd->gmtod', weights, head_values, precision=lax.Precision.HIGHEST)
        attention = lax.optimization_barrier(jnp.sum(mixture * secondary_value_heads, axis=3)) / row_total[..., None]
        return attention.transpose(2, 0, 1, 3).reshape(TOKENS_PER_SHARE, QUERY_HEADS * HEAD_SIZE).astype(jnp.bfloat16)
    attention = lax.map(one_block, jnp.arange(TOKEN_COUNT // TOKENS_PER_SHARE, dtype=jnp.int32))
    attention = attention.reshape(TOKEN_COUNT, QUERY_HEADS * HEAD_SIZE)
    return jnp.dot(attention, out_weight, preferred_element_type=jnp.float32).astype(jnp.bfloat16)
```

```python
import functools
import math

import jax
import jax.numpy as jnp
from jax import lax
from jax.experimental import pallas as pl
from jax.experimental.pallas import tpu as pltpu
from jax.sharding import PartitionSpec as P

HEAD = 128
FIRST = 512
SECOND = 16
LOG2E = 1.4426950408889634
NEG = -1e30


def core_swap(value, count):
    return lax.ppermute(value, "ctx", [(s, s ^ 1) for s in range(count)])


def chip_shift(value, count, even, odd):
    pairs = [(s, s + 2 * (even if s % 2 == 0 else odd)) for s in range(count)]
    return lax.ppermute(value, "ctx", [(a, b) for a, b in pairs if b < count])


def head_swap(value):
    return lax.ppermute(value, "head", [(0, 1), (1, 0)])


def attend_kernel(
    where_ref, q_ref, k_ref, v_ref, ks_ref, vs_ref, x1_ref, y_ref, yp_ref, z_ref, zp_ref, w_hbm,
    mine_ref, other_ref,
    kbuf, vbuf, vt, ksw, svw, acc, att, wbuf, sem,
):
    shard = where_ref[0]
    core = where_ref[1]
    side = where_ref[2]
    rows = q_ref.shape[0]
    kv_heads = k_ref.shape[1] // HEAD
    group = q_ref.shape[1] // k_ref.shape[1]
    half = w_hbm.shape[1] // 2
    reach = FIRST + rows
    lanes = SECOND * rows

    def w_copy(slot, which):
        cols = pl.ds(pl.multiple_of(which * half, 128), half)
        return pltpu.make_async_copy(w_hbm.at[:, cols], wbuf.at[slot], sem.at[slot])

    w_copy(0, 1 - side).start()
    w_copy(1, side).start()

    first_block = shard - core - FIRST // rows
    key_row = jnp.broadcast_to(k_ref[0:1, :], (rows, k_ref.shape[1]))

    def place(block, keys, values):
        good = first_block + block >= 0
        at = pl.ds(pl.multiple_of(block * rows, rows), rows)
        kbuf[at, :] = jnp.where(good, keys, key_row)
        vbuf[at, :] = jnp.where(good, values, jnp.zeros_like(values))

    def place_chip(pair, flip, ref, stride):
        for slot in range(2):
            block = 2 * pair + jnp.where(flip == 1, 1 - slot, slot)
            at = slot * stride
            place(block, ref[at : at + rows, :], ref[at + rows : at + 2 * rows, :])

    tall = y_ref.shape[0] // 2
    place_chip(3 - core, core, y_ref, tall)
    place_chip(2 + core, 1 - core, yp_ref, tall)
    place_chip(1 - core, core, z_ref, 2 * rows)
    place_chip(core, 1 - core, zp_ref, 2 * rows)
    place(8 + core, k_ref[...], v_ref[...])
    place(9 - core, x1_ref[0:rows, :], x1_ref[rows : 2 * rows, :])

    window = pl.ds(pl.multiple_of(core * rows, rows), reach)
    col_block = first_block + core + lax.broadcasted_iota(jnp.int32, (16, reach), 1) // rows
    ones = jnp.where(col_block >= 0, 1.0, 0.0).astype(jnp.bfloat16)

    lane = lax.broadcasted_iota(jnp.int32, (HEAD, 128), 1)
    low = lane < rows

    y_tail = tall + 2 * rows
    x_tail = 2 * rows
    for g in range(kv_heads):
        cols = slice(g * HEAD, (g + 1) * HEAD)
        vt[g, 0:HEAD, :] = vbuf[window, cols].T
        vt[g, HEAD : HEAD + 16, :] = ones
        for own, out, offset in ((ks_ref, ksw, 0), (vs_ref, svw, SECOND)):
            near = y_ref[y_tail + offset : y_tail + offset + SECOND, cols].astype(jnp.float32)
            twin = x1_ref[x_tail + offset : x_tail + offset + SECOND, cols].astype(jnp.float32)
            mine = own[:, cols].astype(jnp.float32)
            tail = jnp.where(core == 1, twin, near)
            stand_in = jnp.broadcast_to(mine[0:1, :], tail.shape) if offset == 0 else jnp.zeros_like(tail)
            tail = jnp.where(shard == 0, stand_in, tail)
            rest = jnp.zeros((128 - SECOND - rows, HEAD), jnp.float32)
            tokens = jnp.concatenate([tail, mine, rest], axis=0).T
            for pair in range(SECOND // 2):
                near_part = pltpu.roll(tokens, (128 - (2 * pair + 1)) % 128, 1)
                far_part = pltpu.roll(tokens, (rows - (2 * pair + 2)) % 128, 1)
                out[g, :, pair * 128 : (pair + 1) * 128] = jnp.where(low, near_part, far_part)

    width = 256
    key_id = lax.broadcasted_iota(jnp.int32, (rows, width), 0)
    token_id = lax.broadcasted_iota(jnp.int32, (rows, width), 1) % rows
    mask_own = jnp.where(key_id <= token_id, 0.0, NEG)
    mask_far = jnp.where(key_id > token_id, 0.0, NEG)
    scale = LOG2E / math.sqrt(HEAD)

    pair_lane = lax.broadcasted_iota(jnp.int32, (1, 128), 1)

    def one_head(h, _):
        g = h // group
        cols = pl.ds(pl.multiple_of(h * HEAD, HEAD), HEAD)
        q = q_ref[:, cols].astype(jnp.float32) * scale
        qt = jnp.concatenate([q, q], axis=0).T
        qt2 = jnp.concatenate([qt] * (width // 128), axis=1)
        keys = kbuf[window, pl.ds(pl.multiple_of(g * HEAD, HEAD), HEAD)]
        values = vt[g]
        tops, totals = [], []
        for c in range(lanes // width):
            at = slice(c * width, (c + 1) * width)
            products = (qt2 * ksw[g, :, at]).astype(jnp.bfloat16)
            s = jnp.dot(keys, products, preferred_element_type=jnp.float32)
            far = s[:rows] + mask_far
            mid = s[rows : reach - rows]
            own = s[reach - rows :] + mask_own
            top = jnp.maximum(jnp.max(mid, axis=0, keepdims=True), jnp.max(own, axis=0, keepdims=True))
            top = jnp.maximum(top, jnp.max(far, axis=0, keepdims=True))
            weights = jnp.concatenate(
                [jnp.exp2(part - top).astype(jnp.bfloat16) for part in (far, mid, own)], axis=0
            )
            mixed = jnp.dot(values, weights, preferred_element_type=jnp.float32)
            acc[:, at] = mixed[:HEAD] * svw[g, :, at]
            tops.append(top)
            totals.append(mixed[HEAD : HEAD + 1])
        top = jnp.concatenate(tops, axis=1)
        total = jnp.concatenate(totals, axis=1)
        tiles = [slice(i * 128, (i + 1) * 128) for i in range(lanes // 128)]
        peak = functools.reduce(jnp.maximum, [top[:, t] for t in tiles])
        peak = jnp.maximum(peak, pltpu.roll(peak, rows, 1))
        out = jnp.zeros((HEAD, 128), jnp.float32)
        norm = jnp.zeros((1, 128), jnp.float32)
        for i, t in enumerate(tiles):
            offset = 2 * i + pair_lane // rows
            fine = (shard > 0) | (pair_lane % rows + offset >= SECOND - 1)
            grow = jnp.exp2(top[:, t] - peak)
            out = out + acc[:, t] * grow
            norm = norm + jnp.where(fine, total[:, t] * grow, 0.0)
        out = out + pltpu.roll(out, rows, 1)
        norm = norm + pltpu.roll(norm, rows, 1)
        att[:, cols] = (out / norm).T[:rows].astype(jnp.bfloat16)
        return 0

    lax.fori_loop(0, kv_heads * group, one_head, 0)

    w_copy(0, 1 - side).wait()
    other_ref[...] = jnp.dot(att[...], wbuf[0], preferred_element_type=jnp.float32).astype(jnp.bfloat16)
    w_copy(1, side).wait()
    mine_ref[...] = jnp.dot(att[...], wbuf[1], preferred_element_type=jnp.float32)


def attend(where, *arrays):
    queries, keys, out_weight = arrays[0], arrays[1], arrays[-1]
    rows, wide = queries.shape
    narrow = keys.shape[1]
    kv_heads = narrow // HEAD
    depth, features = out_weight.shape
    reach, lanes = FIRST + rows, SECOND * rows
    vmem = pl.BlockSpec(memory_space=pltpu.VMEM)
    return pl.pallas_call(
        attend_kernel,
        out_shape=(
            jax.ShapeDtypeStruct((rows, features // 2), jnp.float32),
            jax.ShapeDtypeStruct((rows, features // 2), jnp.bfloat16),
        ),
        in_specs=[pl.BlockSpec(memory_space=pltpu.SMEM)]
        + [vmem] * (len(arrays) - 1)
        + [pl.BlockSpec(memory_space=pl.ANY)],
        out_specs=(vmem, vmem),
        scratch_shapes=[
            pltpu.VMEM((reach + rows, narrow), jnp.bfloat16),
            pltpu.VMEM((reach + rows, narrow), jnp.bfloat16),
            pltpu.VMEM((kv_heads, HEAD + 16, reach), jnp.bfloat16),
            pltpu.VMEM((kv_heads, HEAD, lanes), jnp.float32),
            pltpu.VMEM((kv_heads, HEAD, lanes), jnp.float32),
            pltpu.VMEM((HEAD, lanes), jnp.float32),
            pltpu.VMEM((rows, wide), jnp.bfloat16),
            pltpu.VMEM((2, depth, features // 2), jnp.bfloat16),
            pltpu.SemaphoreType.DMA((2,)),
        ],
        compiler_params=pltpu.CompilerParams(vmem_limit_bytes=40 << 20),
        name="attend",
    )(where, *arrays)


def body(queries, keys_first, primary_value_array, keys_second, secondary_value_array, out_weight):
    count = lax.axis_size("ctx")
    rows = queries.shape[0]
    shard = lax.axis_index("ctx")
    where = jnp.stack([shard, shard % 2, lax.axis_index("head")]).astype(jnp.int32)
    packed = jnp.concatenate(
        [
            keys_first,
            primary_value_array,
            keys_second[rows - SECOND :],
            secondary_value_array[rows - SECOND :],
        ],
        axis=0,
    )
    twin = core_swap(packed, count)
    near_load = jnp.concatenate([packed, twin], axis=0)
    far_load = jnp.concatenate([packed[: 2 * rows], twin[: 2 * rows]], axis=0)
    near = chip_shift(near_load, count, 1, 2)
    far = chip_shift(far_load, count, 3, 4)
    near_twin = core_swap(near, count)
    far_twin = core_swap(far, count)
    mine, other = attend(
        where,
        queries,
        keys_first,
        primary_value_array,
        keys_second,
        secondary_value_array,
        twin,
        near,
        near_twin,
        far,
        far_twin,
        out_weight,
    )
    return (mine + head_swap(other).astype(jnp.float32)).astype(jnp.bfloat16)


def solution(mesh):
    in_specs = (P("ctx", "head"),) * 5 + (P("head", None),)
    return jax.shard_map(body, mesh=mesh, in_specs=in_specs, out_specs=P("ctx", "head"), check_vma=False)
```

```python
import functools
import math

import jax
import jax.numpy as jnp
from jax import lax
from jax.experimental import pallas as pl
from jax.experimental.pallas import tpu as pltpu
from jax.sharding import PartitionSpec as P


HEAD = 128
FIRST = 512
SECOND = 16
LOG2E = 1.4426950408889634
NEG = -1e30
WIDTH = 256
ANY = pl.BlockSpec(memory_space=pl.ANY)
VMEM = pl.BlockSpec(memory_space=pltpu.VMEM)
SMEM = pl.BlockSpec(memory_space=pltpu.SMEM)
GRANT = pltpu.CompilerParams(vmem_limit_bytes=20 << 20)
SMALL = pltpu.CompilerParams(vmem_limit_bytes=2 << 20)


def core_swap(value, count):
    return lax.ppermute(value, "ctx", [(s, s ^ 1) for s in range(count)])


def chip_shift(value, count, even, odd):
    pairs = [(s, s + 2 * (even if s % 2 == 0 else odd)) for s in range(count)]
    return lax.ppermute(value, "ctx", [(a, b) for a, b in pairs if b < count])


def head_swap(value):
    return lax.ppermute(value, "head", [(0, 1), (1, 0)])


def pack_kernel(k_ref, v_ref, ks_ref, vs_ref, out_ref, sem):
    rows = k_ref.shape[0]
    tail = pl.ds(rows - SECOND, SECOND)
    parts = (
        (k_ref, out_ref.at[pl.ds(0, rows)]),
        (v_ref, out_ref.at[pl.ds(rows, rows)]),
        (ks_ref.at[tail], out_ref.at[pl.ds(2 * rows, SECOND)]),
        (vs_ref.at[tail], out_ref.at[pl.ds(2 * rows + SECOND, SECOND)]),
    )
    copies = [pltpu.make_async_copy(a, b, sem.at[i]) for i, (a, b) in enumerate(parts)]
    for copy in copies:
        copy.start()
    for copy in copies:
        copy.wait()


def pack(k, v, ks, vs):
    rows, wide = k.shape
    return pl.pallas_call(
        pack_kernel,
        out_shape=jax.ShapeDtypeStruct((2 * rows + 2 * SECOND, wide), k.dtype),
        in_specs=[ANY] * 4,
        out_specs=VMEM,
        scratch_shapes=[pltpu.SemaphoreType.DMA((4,))],
        compiler_params=SMALL,
        name="pack",
    )(k, v, ks, vs)


def join_kernel(own_ref, twin_ref, near_ref, far_ref):
    tall = own_ref.shape[0]
    short = far_ref.shape[0] // 2
    near_ref[0:tall] = own_ref[...]
    near_ref[tall : 2 * tall] = twin_ref[...]
    far_ref[0:short] = own_ref[0:short]
    far_ref[short : 2 * short] = twin_ref[0:short]


def join(own, twin):
    tall, wide = own.shape
    return pl.pallas_call(
        join_kernel,
        out_shape=(
            jax.ShapeDtypeStruct((2 * tall, wide), own.dtype),
            jax.ShapeDtypeStruct((2 * (tall - 2 * SECOND), wide), own.dtype),
        ),
        in_specs=[VMEM] * 2,
        out_specs=(VMEM, VMEM),
        compiler_params=SMALL,
        name="join",
    )(own, twin)


def windows(where_ref, ks, vs, x1, y, ksw, svw, kv_heads, rows):
    shard, core = where_ref[0], where_ref[1]
    lanes = SECOND * rows
    tall = y.shape[0] // 2
    token = lax.broadcasted_iota(jnp.int32, (128, lanes), 0)
    pair = lax.broadcasted_iota(jnp.int32, (128, lanes), 1)
    pick = (token == pair % rows + pair // rows + 1).astype(jnp.bfloat16)
    for own, out, at in ((ks, ksw, 0), (vs, svw, SECOND)):
        near = y[tall + 2 * rows + at : tall + 2 * rows + at + SECOND, :]
        twin = x1[2 * rows + at : 2 * rows + at + SECOND, :]
        mine = own[...].astype(jnp.float32)
        tail = jnp.where(core == 1, twin.astype(jnp.float32), near.astype(jnp.float32))
        tail = jnp.where(shard == 0, jnp.zeros_like(tail), tail)
        rest = jnp.zeros((128 - SECOND - rows, mine.shape[1]), jnp.float32)
        tokens = jnp.concatenate([tail, mine, rest], axis=0)
        for g in range(kv_heads):
            turned = tokens[:, g * HEAD : (g + 1) * HEAD].T.astype(jnp.bfloat16)
            out[g] = jnp.dot(turned, pick, preferred_element_type=jnp.float32).astype(out.dtype)


def turn_queries(q, qt, heads):
    scale = LOG2E / math.sqrt(HEAD)
    for h in range(heads):
        part = q[:, h * HEAD : (h + 1) * HEAD].astype(jnp.float32) * scale
        qt[h] = jnp.concatenate([part, part], axis=0).T


def stage_masks(where_ref, kcat, paug, start, span, first_block, mask_at, later_ok, rows, kv_heads):
    lanes = SECOND * rows
    row = lax.broadcasted_iota(jnp.int32, (span, HEAD), 0)
    col = lax.broadcasted_iota(jnp.int32, (span, HEAD), 1)
    gone = jnp.where(first_block + row // rows < 0, NEG, 0.0)
    extra = jnp.where(col == rows, gone, jnp.where(col == rows + 1, 1.0, 0.0))
    extra = jnp.where((col < rows) & (row - mask_at == col), 1.0, extra).astype(jnp.bfloat16)
    window = pl.ds(pl.multiple_of(start, rows), span)
    for g in range(kv_heads):
        kcat[g, window, HEAD : 2 * HEAD] = extra
    feature = lax.broadcasted_iota(jnp.int32, (HEAD, lanes), 0)
    pair = lax.broadcasted_iota(jnp.int32, (HEAD, lanes), 1)
    token = pair % rows
    hidden = (feature <= token) if later_ok else (feature > token)
    bias = jnp.where((feature < rows) & hidden, NEG, 0.0)
    bias = jnp.where(feature == rows, 1.0, bias)
    early = (where_ref[0] == 0) & (token + pair // rows < SECOND - 1)
    bias = jnp.where((feature == rows + 1) & early, NEG, bias)
    paug[...] = bias.astype(jnp.bfloat16)


def stage_values(vbuf, vt, start, span, rows, kv_heads):
    window = pl.ds(pl.multiple_of(start, rows), span)
    for g in range(kv_heads):
        vt[g] = vbuf[window, g * HEAD : (g + 1) * HEAD].T


def run_heads(kcat, start, span, qt, ksw, svw, paug, vt, sbufs, wbufs, tops, totals, acc, stat, group, heads, rows, finish):
    lanes = SECOND * rows
    chunks = lanes // WIDTH
    window = pl.ds(pl.multiple_of(start, rows), span)

    def score(h, c):
        g = h // group
        at = slice(c * WIDTH, (c + 1) * WIDTH)
        q = qt[h]
        products = jnp.concatenate([q] * (WIDTH // 128), axis=1) * ksw[g, :, at].astype(jnp.float32)
        products = jnp.concatenate([products.astype(jnp.bfloat16), paug[:, at]], axis=0)
        s = jnp.dot(kcat[g, window, :], products, preferred_element_type=jnp.float32)
        sbufs[c % 2][...] = s
        tops[c % 2][...] = jnp.max(s, axis=0, keepdims=True)

    def soften(c):
        e = jnp.exp2(sbufs[c % 2][...] - tops[c % 2][...])
        wbufs[c % 2][...] = e.astype(jnp.bfloat16)
        totals[c % 2][0:1, :] = jnp.sum(e, axis=0, keepdims=True)
        totals[c % 2][1:2, :] = tops[c % 2][...]

    def mix(h, c):
        g = h // group
        at = slice(c * WIDTH, (c + 1) * WIDTH)
        mixed = jnp.dot(vt[g], wbufs[c % 2][...], preferred_element_type=jnp.float32)
        acc[h % 2, :, at] = mixed * svw[g, :, at].astype(jnp.float32)
        stat[h % 2, :, at] = totals[c % 2][...]

    def combine(h):
        slot = h % 2
        tiles = [slice(i * 128, (i + 1) * 128) for i in range(lanes // 128)]
        top = [stat[slot, 1:2, t] for t in tiles]
        peak = functools.reduce(jnp.maximum, top)
        peak = jnp.maximum(peak, pltpu.roll(peak, rows, 1))
        out, norm = None, None
        for i, t in enumerate(tiles):
            grow = jnp.exp2(top[i] - peak)
            more, plus = acc[slot, :, t] * grow, stat[slot, 0:1, t] * grow
            out, norm = (more, plus) if out is None else (out + more, norm + plus)
        out = out + pltpu.roll(out, rows, 1)
        norm = norm + pltpu.roll(norm, rows, 1)
        finish(h, out, peak, norm)

    def one_head(h, _):
        later = jnp.minimum(h + 1, heads - 1)
        combine(jnp.maximum(h - 1, 0))
        for c in range(chunks):
            mix(h, c)
            soften((c + 1) % chunks)
            score(h if c + 2 < chunks else later, (c + 2) % chunks)
        return 0

    acc[...] = jnp.zeros_like(acc)
    stat[...] = jnp.zeros_like(stat)
    score(0, 0)
    score(0, 1)
    soften(0)
    lax.fori_loop(0, heads, one_head, 0)
    combine(heads - 1)


def start_all(pairs, sem):
    copies = [pltpu.make_async_copy(a, b, sem.at[i]) for i, (a, b) in enumerate(pairs)]
    for copy in copies:
        copy.start()
    return copies


def block_copies(ref, row, rows, block, kcat, vbuf):
    at = pl.ds(pl.multiple_of(block * rows, rows), rows)
    keys = ref.at[pl.ds(row, rows)]
    pairs = [(keys.at[:, pl.ds(g * HEAD, HEAD)], kcat.at[g, at, pl.ds(0, HEAD)]) for g in range(kcat.shape[0])]
    return pairs + [(ref.at[pl.ds(row + rows, rows)], vbuf.at[at])]


def chip_blocks(ref, stride, rows, pair, flip, kcat, vbuf):
    pairs = []
    for slot in range(2):
        block = 2 * pair + jnp.where(flip == 1, 1 - slot, slot)
        pairs += block_copies(ref, slot * stride, rows, block, kcat, vbuf)
    return pairs


def near_kernel(
    where_ref, q_hbm, x0_hbm, ks_hbm, vs_hbm, x1_hbm, y_hbm, yp_hbm,
    out_ref, peak_ref, norm_ref, ksw, svw, qt,
    q, ks, vs, x1, y, kcat, vbuf, vt, paug, s0, s1, w0, w1, t0, t1, n0, n1, acc, stat, sem,
):
    shard, core = where_ref[0], where_ref[1]
    rows, wide = q_hbm.shape
    kv_heads, heads = kcat.shape[0], wide // HEAD
    blocks = vbuf.shape[0] // rows
    span = (blocks - 1) * rows
    tall = y_hbm.shape[0] // 2
    pairs = [(q_hbm, q), (ks_hbm, ks), (vs_hbm, vs), (x1_hbm, x1), (y_hbm, y)]
    pairs += block_copies(x0_hbm, 0, rows, blocks - 2 + core, kcat, vbuf)
    pairs += block_copies(x1_hbm, 0, rows, blocks - 1 - core, kcat, vbuf)
    pairs += chip_blocks(y_hbm, tall, rows, 1 - core, core, kcat, vbuf)
    pairs += chip_blocks(yp_hbm, tall, rows, core, 1 - core, kcat, vbuf)
    copies = start_all(pairs, sem)
    start = core * rows
    stage_masks(where_ref, kcat, paug, start, span, shard - (blocks - 2), span - rows, False, rows, kv_heads)
    for copy in copies:
        copy.wait()
    windows(where_ref, ks, vs, x1, y, ksw, svw, kv_heads, rows)
    turn_queries(q, qt, heads)
    stage_values(vbuf, vt, start, span, rows, kv_heads)

    def finish(h, out, peak, norm):
        out_ref[h] = out
        peak_ref[h] = jnp.broadcast_to(peak, (8, 128))
        norm_ref[h] = jnp.broadcast_to(norm, (8, 128))

    run_heads(
        kcat, start, span, qt, ksw, svw, paug, vt, (s0, s1), (w0, w1), (t0, t1), (n0, n1), acc, stat,
        heads // kv_heads, heads, rows, finish,
    )


def far_kernel(
    where_ref, y_hbm, z_hbm, zp_hbm, acc1_ref, peak1_ref, norm1_ref, ksw, svw, qt, w_hbm,
    mine_ref, other_ref,
    kcat, vbuf, vt, paug, s0, s1, w0, w1, t0, t1, n0, n1, acc, stat, att, wbuf, sem, wsem,
):
    shard, core, side = where_ref[0], where_ref[1], where_ref[2]
    rows, wide = att.shape
    kv_heads, heads = kcat.shape[0], wide // HEAD
    half = w_hbm.shape[1] // 2
    blocks = vbuf.shape[0] // rows
    span = (blocks - 1) * rows
    tall = y_hbm.shape[0] // 2
    pairs = chip_blocks(z_hbm, 2 * rows, rows, 1 - core, core, kcat, vbuf)
    pairs += chip_blocks(zp_hbm, 2 * rows, rows, core, 1 - core, kcat, vbuf)
    pairs += block_copies(y_hbm, tall, rows, blocks - 1, kcat, vbuf)
    copies = start_all(pairs, sem)

    def w_copy(slot, which):
        cols = pl.ds(pl.multiple_of(which * half, 128), half)
        return pltpu.make_async_copy(w_hbm.at[:, cols], wbuf.at[slot], wsem.at[slot])

    w_copy(0, 1 - side).start()
    w_copy(1, side).start()
    start = core * rows
    stage_masks(where_ref, kcat, paug, start, span, shard - FIRST // rows, 0, True, rows, kv_heads)
    for copy in copies:
        copy.wait()
    stage_values(vbuf, vt, start, span, rows, kv_heads)

    def finish(h, out, peak, norm):
        before = peak1_ref[h][0:1]
        both = jnp.maximum(peak, before)
        grow, grow1 = jnp.exp2(peak - both), jnp.exp2(before - both)
        norm = norm * grow + norm1_ref[h][0:1] * grow1
        out = (out * grow + acc1_ref[h] * grow1) / norm
        att[:, pl.ds(pl.multiple_of(h * HEAD, HEAD), HEAD)] = out.T[:rows].astype(jnp.bfloat16)

    run_heads(
        kcat, start, span, qt, ksw, svw, paug, vt, (s0, s1), (w0, w1), (t0, t1), (n0, n1), acc, stat,
        heads // kv_heads, heads, rows, finish,
    )
    w_copy(0, 1 - side).wait()
    other_ref[...] = jnp.dot(att[...], wbuf[0], preferred_element_type=jnp.float32).astype(jnp.bfloat16)
    w_copy(1, side).wait()
    mine_ref[...] = jnp.dot(att[...], wbuf[1], preferred_element_type=jnp.float32)


def common_scratch(rows, kv_heads, blocks):
    lanes, span = SECOND * rows, (blocks - 1) * rows
    return [
        pltpu.VMEM((kv_heads, blocks * rows, 2 * HEAD), jnp.bfloat16),
        pltpu.VMEM((blocks * rows, kv_heads * HEAD), jnp.bfloat16),
        pltpu.VMEM((kv_heads, HEAD, span), jnp.bfloat16),
        pltpu.VMEM((HEAD, lanes), jnp.bfloat16),
        pltpu.VMEM((span, WIDTH), jnp.float32),
        pltpu.VMEM((span, WIDTH), jnp.float32),
        pltpu.VMEM((span, WIDTH), jnp.bfloat16),
        pltpu.VMEM((span, WIDTH), jnp.bfloat16),
        pltpu.VMEM((1, WIDTH), jnp.float32),
        pltpu.VMEM((1, WIDTH), jnp.float32),
        pltpu.VMEM((2, WIDTH), jnp.float32),
        pltpu.VMEM((2, WIDTH), jnp.float32),
        pltpu.VMEM((2, HEAD, lanes), jnp.float32),
        pltpu.VMEM((2, 2, lanes), jnp.float32),
    ]


def attend_near(where, q, x0, ks, vs, x1, y, yp):
    rows, wide = q.shape
    kv_heads, heads, lanes = ks.shape[1] // HEAD, wide // HEAD, SECOND * rows
    return pl.pallas_call(
        near_kernel,
        out_shape=(
            jax.ShapeDtypeStruct((heads, HEAD, 128), jnp.float32),
            jax.ShapeDtypeStruct((heads, 8, 128), jnp.float32),
            jax.ShapeDtypeStruct((heads, 8, 128), jnp.float32),
            jax.ShapeDtypeStruct((kv_heads, HEAD, lanes), jnp.bfloat16),
            jax.ShapeDtypeStruct((kv_heads, HEAD, lanes), jnp.bfloat16),
            jax.ShapeDtypeStruct((heads, HEAD, 128), jnp.float32),
        ),
        in_specs=[SMEM] + [ANY] * 7,
        out_specs=(VMEM,) * 6,
        scratch_shapes=[pltpu.VMEM(a.shape, a.dtype) for a in (q, ks, vs, x1, y)]
        + common_scratch(rows, kv_heads, 6)
        + [pltpu.SemaphoreType.DMA((23,))],
        compiler_params=GRANT,
        cost_estimate=pl.CostEstimate(flops=8_000_000_000, transcendentals=4_000_000, bytes_accessed=16_000_000),
        name="near",
    )(where, q, x0, ks, vs, x1, y, yp)


def attend_far(where, y, z, zp, acc1, peak1, norm1, ksw, svw, qt, w):
    kv_heads, heads = ksw.shape[0], qt.shape[0]
    rows = ksw.shape[2] // SECOND
    depth, features = w.shape
    return pl.pallas_call(
        far_kernel,
        out_shape=(
            jax.ShapeDtypeStruct((rows, features // 2), jnp.float32),
            jax.ShapeDtypeStruct((rows, features // 2), jnp.bfloat16),
        ),
        in_specs=[SMEM] + [ANY] * 3 + [VMEM] * 6 + [ANY],
        out_specs=(VMEM, VMEM),
        scratch_shapes=common_scratch(rows, kv_heads, 5)
        + [
            pltpu.VMEM((rows, heads * HEAD), jnp.bfloat16),
            pltpu.VMEM((2, depth, features // 2), jnp.bfloat16),
            pltpu.SemaphoreType.DMA((15,)),
            pltpu.SemaphoreType.DMA((2,)),
        ],
        compiler_params=GRANT,
        name="far",
    )(where, y, z, zp, acc1, peak1, norm1, ksw, svw, qt, w)


def body(queries, keys_first, primary_value_array, keys_second, secondary_value_array, out_weight):
    count = lax.axis_size("ctx")
    queries, keys_first, primary_value_array, keys_second, secondary_value_array, out_weight = (
        pltpu.with_memory_space_constraint(a, pltpu.HBM)
        for a in (queries, keys_first, primary_value_array, keys_second, secondary_value_array, out_weight)
    )
    shard = lax.axis_index("ctx")
    where = jnp.stack([shard, shard % 2, lax.axis_index("head")]).astype(jnp.int32)
    packed = pack(keys_first, primary_value_array, keys_second, secondary_value_array)
    twin = core_swap(packed, count)
    near_load, far_load = join(packed, twin)
    near = chip_shift(near_load, count, 1, 2)
    far = chip_shift(far_load, count, 3, 4)
    near_twin = core_swap(near, count)
    sums = attend_near(where, queries, packed, keys_second, secondary_value_array, twin, near, near_twin)
    far_twin = core_swap(far, count)
    mine, other = attend_far(where, near, far, far_twin, *sums, out_weight)
    other = head_swap(other)
    return (mine + other.astype(jnp.float32)).astype(jnp.bfloat16)


def solution(mesh):
    in_specs = (P("ctx", "head"),) * 5 + (P("head", None),)
    return jax.shard_map(body, mesh=mesh, in_specs=in_specs, out_specs=P("ctx", "head"), check_vma=False)
```

```python
import functools
import math

import jax
import jax.numpy as jnp
from jax import lax
from jax.experimental import pallas as pl
from jax.experimental.pallas import tpu as pltpu
from jax.sharding import PartitionSpec as P


HEAD = 128
FIRST = 512
SECOND = 16
LOG2E = 1.4426950408889634
NEG = -1e30
WIDTH = 256
UNROLL = 4
NEAR = 5
ANY = pl.BlockSpec(memory_space=pl.ANY)
VMEM = pl.BlockSpec(memory_space=pltpu.VMEM)
SMEM = pl.BlockSpec(memory_space=pltpu.SMEM)
GRANT = pltpu.CompilerParams(vmem_limit_bytes=20 << 20)
SMALL = pltpu.CompilerParams(vmem_limit_bytes=2 << 20)


def core_swap(value, count):
    return lax.ppermute(value, "ctx", [(s, s ^ 1) for s in range(count)])


def chip_shift(value, count, even, odd):
    pairs = [(s, s + 2 * (even if s % 2 == 0 else odd)) for s in range(count)]
    return lax.ppermute(value, "ctx", [(a, b) for a, b in pairs if b < count])


def head_swap(value):
    return lax.ppermute(value, "head", [(0, 1), (1, 0)])


def pack_kernel(k_ref, v_ref, ks_ref, vs_ref, out_ref, sem):
    rows = k_ref.shape[0]
    tail = pl.ds(rows - SECOND, SECOND)
    parts = (
        (k_ref, out_ref.at[pl.ds(0, rows)]),
        (v_ref, out_ref.at[pl.ds(rows, rows)]),
        (ks_ref.at[tail], out_ref.at[pl.ds(2 * rows, SECOND)]),
        (vs_ref.at[tail], out_ref.at[pl.ds(2 * rows + SECOND, SECOND)]),
    )
    copies = [pltpu.make_async_copy(a, b, sem.at[i]) for i, (a, b) in enumerate(parts)]
    for copy in copies:
        copy.start()
    for copy in copies:
        copy.wait()


def pack(k, v, ks, vs):
    rows, wide = k.shape
    return pl.pallas_call(
        pack_kernel,
        out_shape=jax.ShapeDtypeStruct((2 * rows + 2 * SECOND, wide), k.dtype),
        in_specs=[ANY] * 4,
        out_specs=VMEM,
        scratch_shapes=[pltpu.SemaphoreType.DMA((4,))],
        compiler_params=SMALL,
        name="pack",
    )(k, v, ks, vs)


def join_kernel(own_ref, twin_ref, near_ref, far_ref):
    short = far_ref.shape[0] // 2
    for ref in (near_ref, far_ref):
        ref[0:short] = own_ref[0:short]
        ref[short : 2 * short] = twin_ref[0:short]
    near_ref[2 * short :] = twin_ref[short:]


def join(own, twin):
    tall, wide = own.shape
    short = tall - 2 * SECOND
    return pl.pallas_call(
        join_kernel,
        out_shape=(
            jax.ShapeDtypeStruct((tall + short, wide), own.dtype),
            jax.ShapeDtypeStruct((2 * short, wide), own.dtype),
        ),
        in_specs=[VMEM] * 2,
        out_specs=(VMEM, VMEM),
        compiler_params=SMALL,
        name="join",
    )(own, twin)


def lane_token(lane):
    few = WIDTH // SECOND
    return few * (lane // WIDTH) + lane % few, (lane % WIDTH) // few


def prep_kernel(where_ref, q_hbm, qt_ref, pick_ref, near_bias_ref, far_bias_ref, near_extra_ref, far_extra_ref, q, sem):
    shard = where_ref[0]
    copy = pltpu.make_async_copy(q_hbm, q, sem)
    copy.start()
    rows = q.shape[0]
    shape = pick_ref.shape
    feature = lax.broadcasted_iota(jnp.int32, shape, 0)
    token, offset = lane_token(lax.broadcasted_iota(jnp.int32, shape, 1))
    pick_ref[...] = (feature == token + offset + 1).astype(jnp.bfloat16)
    early = (shard == 0) & (token + offset < SECOND - 1)
    last = jnp.where(feature == rows, 1.0, jnp.where((feature == rows + 1) & early, NEG, 0.0))
    for ref, hidden in ((near_bias_ref, feature > token), (far_bias_ref, feature <= token)):
        ref[...] = jnp.where((feature < rows) & hidden, NEG, last).astype(jnp.bfloat16)
    for ref, first, cut in (
        (near_extra_ref, shard + 1 - near_extra_ref.shape[0] // rows, near_extra_ref.shape[0] - rows),
        (far_extra_ref, shard - FIRST // rows, 0),
    ):
        row = lax.broadcasted_iota(jnp.int32, ref.shape, 0)
        col = lax.broadcasted_iota(jnp.int32, ref.shape, 1)
        gone = jnp.where(first + row // rows < 0, NEG, 0.0)
        extra = jnp.where(col == rows, gone, jnp.where(col == rows + 1, 1.0, 0.0))
        ref[...] = jnp.where((col < rows) & (row - cut == col), 1.0, extra).astype(jnp.bfloat16)
    copy.wait()
    scale = LOG2E / math.sqrt(HEAD)
    few = WIDTH // SECOND
    for h in range(qt_ref.shape[0]):
        part = q[:, h * HEAD : (h + 1) * HEAD].astype(jnp.float32) * scale
        for c in range(qt_ref.shape[1]):
            qt_ref[h, c] = jnp.concatenate([part[c * few : (c + 1) * few]] * (128 // few), axis=0).T


def prep(where, q):
    rows, wide = q.shape
    heads, lanes, chunks = wide // HEAD, SECOND * rows, SECOND * rows // WIDTH
    return pl.pallas_call(
        prep_kernel,
        out_shape=(
            jax.ShapeDtypeStruct((heads, chunks, HEAD, 128), jnp.float32),
            *[jax.ShapeDtypeStruct((HEAD, lanes), jnp.bfloat16)] * 3,
            jax.ShapeDtypeStruct((NEAR * rows, HEAD), jnp.bfloat16),
            jax.ShapeDtypeStruct((FIRST + rows - NEAR * rows, HEAD), jnp.bfloat16),
        ),
        in_specs=[SMEM, ANY],
        out_specs=(VMEM,) * 6,
        scratch_shapes=[pltpu.VMEM(q.shape, q.dtype), pltpu.SemaphoreType.DMA(())],
        compiler_params=GRANT,
        name="prep",
    )(where, q)


def windows(where_ref, ks, vs, x1, y, pick, ksw, svw, rows):
    shard, core = where_ref[0], where_ref[1]
    for own, out, at in ((ks, ksw, 0), (vs, svw, SECOND)):
        near = y[4 * rows + at : 4 * rows + at + SECOND, :]
        twin = x1[2 * rows + at : 2 * rows + at + SECOND, :]
        mine = own[...].astype(jnp.float32)
        tail = jnp.where(core == 1, twin.astype(jnp.float32), near.astype(jnp.float32))
        tail = jnp.where(shard == 0, jnp.zeros_like(tail), tail)
        rest = jnp.zeros((128 - SECOND - rows, mine.shape[1]), jnp.float32)
        tokens = jnp.concatenate([tail, mine, rest], axis=0)
        for g in range(out.shape[0]):
            turned = tokens[:, g * HEAD : (g + 1) * HEAD].T.astype(jnp.bfloat16)
            out[g] = jnp.dot(turned, pick[...], preferred_element_type=jnp.float32)


def stage(kcat, vbuf, vt, extra, start, span):
    window = pl.ds(pl.multiple_of(start, 16), span)
    for g in range(kcat.shape[0]):
        kcat[g, window, HEAD : 2 * HEAD] = extra[...]
        vt[g] = vbuf[window, g * HEAD : (g + 1) * HEAD].T


def run_heads(kcat, start, qt, ksw, svw, bias, vt, sbuf, wbuf, tops, grows, out, peak, norm, before=None):
    kv_heads = ksw.shape[0]
    heads, chunks = qt.shape[:2]
    group = heads // kv_heads
    steps = group * chunks
    window = pl.ds(pl.multiple_of(start, 16), vt.shape[2])
    tiles = [slice(i * 128, (i + 1) * 128) for i in range(WIDTH // 128)]

    def place(step, g):
        step = jnp.minimum(step, steps - 1)
        c = step // group
        return g * group + step % group, c, pl.ds(pl.multiple_of(c * WIDTH, WIDTH), WIDTH)

    def score(step, turn):
        for g in range(kv_heads):
            h, c, at = place(step, g)
            products = jnp.concatenate([qt[h, c]] * len(tiles), axis=1) * ksw[g, :, at]
            products = jnp.concatenate([products.astype(jnp.bfloat16), bias[:, at]], axis=0)
            s = jnp.dot(kcat[g, window, :], products, preferred_element_type=jnp.float32)
            sbuf[turn][g][...] = s
            top = jnp.max(s, axis=0, keepdims=True)
            tops[turn][g][...] = functools.reduce(jnp.maximum, [top[:, t] for t in tiles])

    def soften(step, turn):
        for g in range(kv_heads):
            h, c, _ = place(step, g)
            top = tops[turn][g][...]
            if before is not None:
                top = jnp.maximum(top, before[1][c, pl.ds(h, 1), :])
                grow = jnp.exp2(before[1][c, pl.ds(h, 1), :] - top)
                grows[turn][g][...] = grow
            e = jnp.exp2(sbuf[turn][g][...] - jnp.concatenate([top] * len(tiles), axis=1))
            wbuf[turn][g][...] = e.astype(jnp.bfloat16)
            total = jnp.sum(e, axis=0, keepdims=True)
            total = functools.reduce(jnp.add, [total[:, t] for t in tiles])
            if before is not None:
                total = total + before[2][c, pl.ds(h, 1), :] * grow
            peak[c, pl.ds(h, 1), :] = top
            norm[c, pl.ds(h, 1), :] = total

    def mix(step, turn):
        for g in range(kv_heads):
            h, c, at = place(step, g)
            mixed = jnp.dot(vt[g], wbuf[turn][g][...], preferred_element_type=jnp.float32)
            mixed = mixed * svw[g, :, at]
            sums = functools.reduce(jnp.add, [mixed[:, t] for t in tiles])
            if before is not None:
                sums = sums + before[0][h, c] * grows[turn][g][...]
            out[h, c] = sums

    def several(i, _):
        for turn in range(UNROLL):
            step = UNROLL * i + turn
            mix(step, turn % 2)
            soften(step + 1, (turn + 1) % 2)
            score(step + 2, turn % 2)
        return 0

    score(0, 0)
    score(1, 1)
    soften(0, 0)
    lax.fori_loop(0, steps // UNROLL, several, 0)


def start_all(pairs, sem):
    copies = [pltpu.make_async_copy(a, b, sem.at[i]) for i, (a, b) in enumerate(pairs)]
    for copy in copies:
        copy.start()
    return copies


def block_copies(ref, row, rows, block, kcat, vbuf):
    at = pl.ds(pl.multiple_of(block * rows, rows), rows)
    keys = ref.at[pl.ds(row, rows)]
    pairs = [(keys.at[:, pl.ds(g * HEAD, HEAD)], kcat.at[g, at, pl.ds(0, HEAD)]) for g in range(kcat.shape[0])]
    return pairs + [(ref.at[pl.ds(row + rows, rows)], vbuf.at[at])]


def chip_blocks(ref, rows, pair, flip, kcat, vbuf):
    pairs = []
    for slot in range(2):
        block = 2 * pair + jnp.where(flip == 1, 1 - slot, slot)
        pairs += block_copies(ref, slot * 2 * rows, rows, block, kcat, vbuf)
    return pairs


def near_kernel(
    where_ref, x0_hbm, ks_hbm, vs_hbm, x1_hbm, y_hbm, yp_hbm, qt, pick, bias, extra,
    out_ref, peak_ref, norm_ref, ksw, svw,
    ks, vs, x1, y, kcat, vbuf, vt, sbuf, wbuf, tops, grows, sem,
):
    core = where_ref[1]
    rows = ks.shape[0]
    blocks = vbuf.shape[0] // rows
    pairs = [(ks_hbm, ks), (vs_hbm, vs), (x1_hbm, x1), (y_hbm, y)]
    pairs += block_copies(x0_hbm, 0, rows, blocks - 2 + core, kcat, vbuf)
    pairs += block_copies(x1_hbm, 0, rows, blocks - 1 - core, kcat, vbuf)
    pairs += chip_blocks(y_hbm, rows, 1 - core, core, kcat, vbuf)
    pairs += chip_blocks(yp_hbm, rows, core, 1 - core, kcat, vbuf)
    for copy in start_all(pairs, sem):
        copy.wait()
    windows(where_ref, ks, vs, x1, y, pick, ksw, svw, rows)
    stage(kcat, vbuf, vt, extra, core * rows, NEAR * rows)
    run_heads(kcat, core * rows, qt, ksw, svw, bias, vt, sbuf, wbuf, tops, grows, out_ref, peak_ref, norm_ref)


def far_kernel(
    where_ref, y_hbm, z_hbm, zp_hbm, acc1_ref, peak1_ref, norm1_ref, ksw, svw, qt, bias, extra, w_hbm,
    other_ref, att,
    kcat, vbuf, vt, sbuf, wbuf, tops, grows, out, peak, norm, weight, sem, wsem,
):
    core, side = where_ref[1], where_ref[2]
    rows = att.shape[0]
    half = w_hbm.shape[1] // 2
    blocks = vbuf.shape[0] // rows
    pairs = chip_blocks(z_hbm, rows, 1 - core, core, kcat, vbuf)
    pairs += chip_blocks(zp_hbm, rows, core, 1 - core, kcat, vbuf)
    pairs += block_copies(y_hbm, 2 * rows, rows, blocks - 1, kcat, vbuf)
    copies = start_all(pairs, sem)
    cols = pl.ds(pl.multiple_of((1 - side) * half, 128), half)
    fetch = pltpu.make_async_copy(w_hbm.at[:, cols], weight, wsem)
    fetch.start()
    for copy in copies:
        copy.wait()
    stage(kcat, vbuf, vt, extra, core * rows, (blocks - 1) * rows)
    run_heads(
        kcat, core * rows, qt, ksw, svw, bias, vt, sbuf, wbuf, tops, grows, out, peak, norm, (acc1_ref, peak1_ref, norm1_ref)
    )
    heads, chunks = qt.shape[:2]
    few = WIDTH // SECOND
    shifts = [few << i for i in range((128 // few).bit_length() - 1)]
    for c in range(chunks):
        top = peak[c]
        most = top
        for shift in shifts:
            most = jnp.maximum(most, pltpu.roll(most, shift, 1))
        grow = jnp.exp2(top - most)
        total = norm[c] * grow
        for shift in shifts:
            total = total + pltpu.roll(total, shift, 1)
        grow = grow / total
        for h in range(heads):
            part = (out[h, c] * grow[h : h + 1]).T
            part = functools.reduce(jnp.add, [part[i : i + few] for i in range(0, 128, few)])
            att[c * few : (c + 1) * few, h * HEAD : (h + 1) * HEAD] = part.astype(jnp.bfloat16)
    fetch.wait()
    other_ref[...] = jnp.dot(att[...], weight[...], preferred_element_type=jnp.float32).astype(jnp.bfloat16)


def own_kernel(where_ref, att, w_hbm, mine_ref, weight, sem):
    half = w_hbm.shape[1] // 2
    cols = pl.ds(pl.multiple_of(where_ref[2] * half, 128), half)
    fetch = pltpu.make_async_copy(w_hbm.at[:, cols], weight, sem)
    fetch.start()
    fetch.wait()
    mine_ref[...] = jnp.dot(att[...], weight[...], preferred_element_type=jnp.float32)


def common_scratch(rows, kv_heads, blocks, span):
    def twice(shape, dtype):
        return [[pltpu.VMEM(shape, dtype)] * kv_heads] * 2

    return [
        pltpu.VMEM((kv_heads, blocks * rows, 2 * HEAD), jnp.bfloat16),
        pltpu.VMEM((blocks * rows, kv_heads * HEAD), jnp.bfloat16),
        pltpu.VMEM((kv_heads, HEAD, span), jnp.bfloat16),
        twice((span, WIDTH), jnp.float32),
        twice((span, WIDTH), jnp.bfloat16),
        twice((1, 128), jnp.float32),
        twice((1, 128), jnp.float32),
    ]


def sums_like(qt):
    heads, chunks = qt.shape[:2]
    return [
        jax.ShapeDtypeStruct((heads, chunks, HEAD, 128), jnp.float32),
        *[jax.ShapeDtypeStruct((chunks, heads, 128), jnp.float32)] * 2,
    ]


def attend_near(where, x0, ks, vs, x1, y, yp, qt, pick, bias, extra):
    rows, lanes = ks.shape[0], pick.shape[1]
    kv_heads = ks.shape[1] // HEAD
    return pl.pallas_call(
        near_kernel,
        out_shape=(*sums_like(qt), *[jax.ShapeDtypeStruct((kv_heads, HEAD, lanes), jnp.float32)] * 2),
        in_specs=[SMEM] + [ANY] * 6 + [VMEM] * 4,
        out_specs=(VMEM,) * 5,
        scratch_shapes=[pltpu.VMEM(a.shape, a.dtype) for a in (ks, vs, x1, y)]
        + common_scratch(rows, kv_heads, NEAR + 1, NEAR * rows)
        + [pltpu.SemaphoreType.DMA((22,))],
        compiler_params=GRANT,
        name="near",
    )(where, x0, ks, vs, x1, y, yp, qt, pick, bias, extra)


def attend_far(where, y, z, zp, acc1, peak1, norm1, ksw, svw, qt, bias, extra, w):
    kv_heads, (heads, chunks) = ksw.shape[0], qt.shape[:2]
    rows = ksw.shape[2] // SECOND
    depth, features = w.shape
    span = extra.shape[0]
    return pl.pallas_call(
        far_kernel,
        out_shape=(
            jax.ShapeDtypeStruct((rows, features // 2), jnp.bfloat16),
            jax.ShapeDtypeStruct((rows, heads * HEAD), jnp.bfloat16),
        ),
        in_specs=[SMEM] + [ANY] * 3 + [VMEM] * 8 + [ANY],
        out_specs=(VMEM, VMEM),
        scratch_shapes=common_scratch(rows, kv_heads, span // rows + 1, span)
        + [
            *(pltpu.VMEM(a.shape, a.dtype) for a in (acc1, peak1, norm1)),
            pltpu.VMEM((depth, features // 2), jnp.bfloat16),
            pltpu.SemaphoreType.DMA((15,)),
            pltpu.SemaphoreType.DMA(()),
        ],
        compiler_params=GRANT,
        name="far",
    )(where, y, z, zp, acc1, peak1, norm1, ksw, svw, qt, bias, extra, w)


def project_own(where, att, w):
    rows, (depth, features) = att.shape[0], w.shape
    return pl.pallas_call(
        own_kernel,
        out_shape=jax.ShapeDtypeStruct((rows, features // 2), jnp.float32),
        in_specs=[SMEM, VMEM, ANY],
        out_specs=VMEM,
        scratch_shapes=[pltpu.VMEM((depth, features // 2), jnp.bfloat16), pltpu.SemaphoreType.DMA(())],
        compiler_params=GRANT,
        name="own",
    )(where, att, w)


def body(queries, keys_first, primary_value_array, keys_second, secondary_value_array, out_weight):
    count = lax.axis_size("ctx")
    queries, keys_first, primary_value_array, keys_second, secondary_value_array, out_weight = (
        pltpu.with_memory_space_constraint(a, pltpu.HBM)
        for a in (queries, keys_first, primary_value_array, keys_second, secondary_value_array, out_weight)
    )
    shard = lax.axis_index("ctx")
    where = jnp.stack([shard, shard % 2, lax.axis_index("head")]).astype(jnp.int32)
    packed = pack(keys_first, primary_value_array, keys_second, secondary_value_array)
    twin = core_swap(packed, count)
    near_load, far_load = join(packed, twin)
    near = chip_shift(near_load, count, 1, 2)
    far = chip_shift(far_load, count, 3, 4)
    qt, pick, near_bias, far_bias, near_extra, far_extra = prep(where, queries)
    near_twin = core_swap(near, count)
    sums = attend_near(
        where, packed, keys_second, secondary_value_array, twin, near, near_twin, qt, pick, near_bias, near_extra
    )
    far_twin = core_swap(far, count)
    other, attention = attend_far(where, near, far, far_twin, *sums, qt, far_bias, far_extra, out_weight)
    other = head_swap(other)
    mine = project_own(where, attention, out_weight)
    return (mine + other.astype(jnp.float32)).astype(jnp.bfloat16)


def solution(mesh):
    in_specs = (P("ctx", "head"),) * 5 + (P("head", None),)
    return jax.shard_map(body, mesh=mesh, in_specs=in_specs, out_specs=P("ctx", "head"), check_vma=False)
```

```python
import functools
import math

import jax
import jax.numpy as jnp
from jax import lax
from jax.experimental import pallas as pl
from jax.experimental.pallas import tpu as pltpu
from jax.sharding import PartitionSpec as P


HEAD = 128
FIRST = 512
SECOND = 16
LOG2E = 1.4426950408889634
NEG = -1e30
WIDTH = 256
UNROLL = 4
FAR = 3
NEAR = 5
ANY = pl.BlockSpec(memory_space=pl.ANY)
VMEM = pl.BlockSpec(memory_space=pltpu.VMEM)
SMEM = pl.BlockSpec(memory_space=pltpu.SMEM)
GRANT = pltpu.CompilerParams(vmem_limit_bytes=20 << 20)
SMALL = pltpu.CompilerParams(vmem_limit_bytes=2 << 20)


def core_swap(value, count):
    return lax.ppermute(value, "ctx", [(s, s ^ 1) for s in range(count)])


def chip_shift(value, count, even, odd):
    pairs = [(s, s + 2 * (even if s % 2 == 0 else odd)) for s in range(count)]
    return lax.ppermute(value, "ctx", [(a, b) for a, b in pairs if b < count])


def head_swap(value):
    return lax.ppermute(value, "head", [(0, 1), (1, 0)])


def pack_kernel(k_ref, v_ref, ks_ref, vs_ref, out_ref, sem):
    rows = k_ref.shape[0]
    tail = pl.ds(rows - SECOND, SECOND)
    parts = (
        (k_ref, out_ref.at[pl.ds(0, rows)]),
        (v_ref, out_ref.at[pl.ds(rows, rows)]),
        (ks_ref.at[tail], out_ref.at[pl.ds(2 * rows, SECOND)]),
        (vs_ref.at[tail], out_ref.at[pl.ds(2 * rows + SECOND, SECOND)]),
    )
    copies = [pltpu.make_async_copy(a, b, sem.at[i]) for i, (a, b) in enumerate(parts)]
    for copy in copies:
        copy.start()
    for copy in copies:
        copy.wait()


def pack(k, v, ks, vs):
    rows, wide = k.shape
    return pl.pallas_call(
        pack_kernel,
        out_shape=jax.ShapeDtypeStruct((2 * rows + 2 * SECOND, wide), k.dtype),
        in_specs=[ANY] * 4,
        out_specs=VMEM,
        scratch_shapes=[pltpu.SemaphoreType.DMA((4,))],
        compiler_params=SMALL,
        name="pack",
    )(k, v, ks, vs)


def join_kernel(own_ref, twin_ref, near_ref, far_ref):
    short = far_ref.shape[0] // 2
    for ref in (near_ref, far_ref):
        ref[0:short] = own_ref[0:short]
        ref[short : 2 * short] = twin_ref[0:short]
    near_ref[2 * short :] = twin_ref[short:]


def join(own, twin):
    tall, wide = own.shape
    short = tall - 2 * SECOND
    return pl.pallas_call(
        join_kernel,
        out_shape=(
            jax.ShapeDtypeStruct((tall + short, wide), own.dtype),
            jax.ShapeDtypeStruct((2 * short, wide), own.dtype),
        ),
        in_specs=[VMEM] * 2,
        out_specs=(VMEM, VMEM),
        compiler_params=SMALL,
        name="join",
    )(own, twin)


def lane_token(lane):
    few = WIDTH // SECOND
    return few * (lane // WIDTH) + lane % few, (lane % WIDTH) // few


def prep_kernel(where_ref, q_hbm, qt_ref, pick_ref, near_bias_ref, far_bias_ref, near_extra_ref, far_extra_ref, q, sem):
    shard = where_ref[0]
    copy = pltpu.make_async_copy(q_hbm, q, sem)
    copy.start()
    rows = q.shape[0]
    shape = pick_ref.shape
    feature = lax.broadcasted_iota(jnp.int32, shape, 0)
    token, offset = lane_token(lax.broadcasted_iota(jnp.int32, shape, 1))
    pick_ref[...] = (feature == token + offset + 1).astype(jnp.bfloat16)
    early = (shard == 0) & (token + offset < SECOND - 1)
    last = jnp.where(feature == rows, 1.0, jnp.where((feature == rows + 1) & early, NEG, 0.0))
    for ref, hidden in ((near_bias_ref, feature > token), (far_bias_ref, feature <= token)):
        ref[...] = jnp.where((feature < rows) & hidden, NEG, last).astype(jnp.bfloat16)
    for ref, first, cut in (
        (near_extra_ref, shard + 1 - near_extra_ref.shape[0] // rows, near_extra_ref.shape[0] - rows),
        (far_extra_ref, shard - FIRST // rows, 0),
    ):
        row = lax.broadcasted_iota(jnp.int32, ref.shape, 0)
        col = lax.broadcasted_iota(jnp.int32, ref.shape, 1)
        gone = jnp.where(first + row // rows < 0, NEG, 0.0)
        extra = jnp.where(col == rows, gone, jnp.where(col == rows + 1, 1.0, 0.0))
        ref[...] = jnp.where((col < rows) & (row - cut == col), 1.0, extra).astype(jnp.bfloat16)
    copy.wait()
    scale = LOG2E / math.sqrt(HEAD)
    few = WIDTH // SECOND
    for h in range(qt_ref.shape[0]):
        part = q[:, h * HEAD : (h + 1) * HEAD].astype(jnp.float32) * scale
        for c in range(qt_ref.shape[1]):
            qt_ref[h, c] = jnp.concatenate([part[c * few : (c + 1) * few]] * (128 // few), axis=0).T


def prep(where, q):
    rows, wide = q.shape
    heads, lanes, chunks = wide // HEAD, SECOND * rows, SECOND * rows // WIDTH
    return pl.pallas_call(
        prep_kernel,
        out_shape=(
            jax.ShapeDtypeStruct((heads, chunks, HEAD, 128), jnp.float32),
            *[jax.ShapeDtypeStruct((HEAD, lanes), jnp.bfloat16)] * 3,
            jax.ShapeDtypeStruct((NEAR * rows, HEAD), jnp.bfloat16),
            jax.ShapeDtypeStruct((FIRST + rows - NEAR * rows, HEAD), jnp.bfloat16),
        ),
        in_specs=[SMEM, ANY],
        out_specs=(VMEM,) * 6,
        scratch_shapes=[pltpu.VMEM(q.shape, q.dtype), pltpu.SemaphoreType.DMA(())],
        compiler_params=GRANT,
        name="prep",
    )(where, q)


def windows(where_ref, ks, vs, x1, y, pick, ksw, svw, rows):
    shard, core = where_ref[0], where_ref[1]
    for own, out, at in ((ks, ksw, 0), (vs, svw, SECOND)):
        near = y[4 * rows + at : 4 * rows + at + SECOND, :]
        twin = x1[2 * rows + at : 2 * rows + at + SECOND, :]
        mine = own[...].astype(jnp.float32)
        tail = jnp.where(core == 1, twin.astype(jnp.float32), near.astype(jnp.float32))
        tail = jnp.where(shard == 0, jnp.zeros_like(tail), tail)
        rest = jnp.zeros((128 - SECOND - rows, mine.shape[1]), jnp.float32)
        tokens = jnp.concatenate([tail, mine, rest], axis=0)
        for g in range(out.shape[0]):
            turned = tokens[:, g * HEAD : (g + 1) * HEAD].T.astype(jnp.bfloat16)
            out[g] = jnp.dot(turned, pick[...], preferred_element_type=jnp.float32)


def stage(kcat, vbuf, vt, extra, start, span):
    window = pl.ds(pl.multiple_of(start, 16), span)
    for g in range(kcat.shape[0]):
        kcat[g, window, HEAD : 2 * HEAD] = extra[...]
        vt[g] = vbuf[window, g * HEAD : (g + 1) * HEAD].T


def run_heads(kcat, start, qt, ksw, svw, bias, vt, sbuf, wbuf, tops, grows, out, peak, norm, span, first=0, before=None):
    kv_heads = ksw.shape[0]
    heads, chunks = out.shape[:2]
    group = heads // kv_heads
    steps = group * chunks
    window = pl.ds(pl.multiple_of(start, 16), span)
    tiles = [slice(i * 128, (i + 1) * 128) for i in range(WIDTH // 128)]

    def place(step, g):
        step = jnp.minimum(step, steps - 1)
        c = first + step // group
        return g * group + step % group, c, pl.ds(pl.multiple_of(c * WIDTH, WIDTH), WIDTH)

    def score(step, turn):
        for g in range(kv_heads):
            h, c, at = place(step, g)
            products = jnp.concatenate([qt[h, c]] * len(tiles), axis=1) * ksw[g, :, at]
            products = jnp.concatenate([products.astype(jnp.bfloat16), bias[:, at]], axis=0)
            s = jnp.dot(kcat[g, window, :], products, preferred_element_type=jnp.float32)
            sbuf[turn][g][...] = s
            top = jnp.max(s, axis=0, keepdims=True)
            tops[turn][g][...] = functools.reduce(jnp.maximum, [top[:, t] for t in tiles])

    def soften(step, turn):
        for g in range(kv_heads):
            h, c, _ = place(step, g)
            top = tops[turn][g][...]
            if before is not None:
                top = jnp.maximum(top, before[1][c, pl.ds(h, 1), :])
                grow = jnp.exp2(before[1][c, pl.ds(h, 1), :] - top)
                grows[turn][g][...] = grow
            e = jnp.exp2(sbuf[turn][g][...] - jnp.concatenate([top] * len(tiles), axis=1))
            wbuf[turn][g][...] = e.astype(jnp.bfloat16)
            total = jnp.sum(e, axis=0, keepdims=True)
            total = functools.reduce(jnp.add, [total[:, t] for t in tiles])
            if before is not None:
                total = total + before[2][c, pl.ds(h, 1), :] * grow
            peak[c - first, pl.ds(h, 1), :] = top
            norm[c - first, pl.ds(h, 1), :] = total

    def mix(step, turn):
        for g in range(kv_heads):
            h, c, at = place(step, g)
            mixed = jnp.dot(vt[g], wbuf[turn][g][...], preferred_element_type=jnp.float32)
            mixed = mixed * svw[g, :, at]
            sums = functools.reduce(jnp.add, [mixed[:, t] for t in tiles])
            if before is not None:
                sums = sums + before[0][h, c] * grows[turn][g][...]
            out[h, c - first] = sums

    def several(i, _):
        for turn in range(UNROLL):
            step = UNROLL * i + turn
            mix(step, turn % 2)
            soften(step + 1, (turn + 1) % 2)
            score(step + 2, turn % 2)
        return 0

    score(0, 0)
    score(1, 1)
    soften(0, 0)
    lax.fori_loop(0, steps // UNROLL, several, 0)


def start_all(pairs, sem):
    copies = [pltpu.make_async_copy(a, b, sem.at[i]) for i, (a, b) in enumerate(pairs)]
    for copy in copies:
        copy.start()
    return copies


def block_copies(ref, row, rows, block, kcat, vbuf):
    at = pl.ds(pl.multiple_of(block * rows, rows), rows)
    keys = ref.at[pl.ds(row, rows)]
    pairs = [(keys.at[:, pl.ds(g * HEAD, HEAD)], kcat.at[g, at, pl.ds(0, HEAD)]) for g in range(kcat.shape[0])]
    return pairs + [(ref.at[pl.ds(row + rows, rows)], vbuf.at[at])]


def chip_blocks(ref, rows, pair, flip, kcat, vbuf):
    pairs = []
    for slot in range(2):
        block = 2 * pair + jnp.where(flip == 1, 1 - slot, slot)
        pairs += block_copies(ref, slot * 2 * rows, rows, block, kcat, vbuf)
    return pairs


def near_kernel(
    where_ref, x0_hbm, ks_hbm, vs_hbm, x1_hbm, y_hbm, yp_hbm, qt, pick, bias, extra,
    out_ref, peak_ref, norm_ref, ksw, svw,
    ks, vs, x1, y, kcat, vbuf, vt, sbuf, wbuf, tops, grows, sem,
):
    core = where_ref[1]
    rows = ks.shape[0]
    blocks = vbuf.shape[0] // rows
    pairs = [(ks_hbm, ks), (vs_hbm, vs), (x1_hbm, x1), (y_hbm, y)]
    pairs += block_copies(x0_hbm, 0, rows, blocks - 2 + core, kcat, vbuf)
    pairs += block_copies(x1_hbm, 0, rows, blocks - 1 - core, kcat, vbuf)
    pairs += chip_blocks(y_hbm, rows, 1 - core, core, kcat, vbuf)
    pairs += chip_blocks(yp_hbm, rows, core, 1 - core, kcat, vbuf)
    for copy in start_all(pairs, sem):
        copy.wait()
    windows(where_ref, ks, vs, x1, y, pick, ksw, svw, rows)
    stage(kcat, vbuf, vt, extra, core * rows, NEAR * rows)
    run_heads(kcat, core * rows, qt, ksw, svw, bias, vt, sbuf, wbuf, tops, grows, out_ref, peak_ref, norm_ref, NEAR * rows)


def finish_heads(out, peak, norm, att):
    heads, chunks = out.shape[:2]
    few = WIDTH // SECOND
    shifts = [few << i for i in range((128 // few).bit_length() - 1)]
    for c in range(chunks):
        top = peak[c]
        most = top
        for shift in shifts:
            most = jnp.maximum(most, pltpu.roll(most, shift, 1))
        grow = jnp.exp2(top - most)
        total = norm[c] * grow
        for shift in shifts:
            total = total + pltpu.roll(total, shift, 1)
        grow = grow / total
        for h in range(heads):
            part = (out[h, c] * grow[h : h + 1]).T
            part = functools.reduce(jnp.add, [part[i : i + few] for i in range(0, 128, few)])
            att[c * few : (c + 1) * few, h * HEAD : (h + 1) * HEAD] = part.astype(jnp.bfloat16)


def far_kernel(
    where_ref, y_hbm, z_hbm, zp_hbm, acc1_ref, peak1_ref, norm1_ref, ksw, svw, qt, bias, extra, w_hbm,
    other_ref, att, kcat, vt, weight, own_weight,
    vbuf, sbuf, wbuf, tops, grows, out, peak, norm, sem, wsem,
):
    core, side = where_ref[1], where_ref[2]
    span = extra.shape[0]
    rows = vbuf.shape[0] - span
    half = w_hbm.shape[1] // 2
    blocks = vbuf.shape[0] // rows
    pairs = chip_blocks(z_hbm, rows, 1 - core, core, kcat, vbuf)
    pairs += chip_blocks(zp_hbm, rows, core, 1 - core, kcat, vbuf)
    pairs += block_copies(y_hbm, 2 * rows, rows, blocks - 1, kcat, vbuf)
    copies = start_all(pairs, sem)
    fetches = []
    for i, (which, to) in enumerate(((1 - side, weight), (side, own_weight))):
        cols = pl.ds(pl.multiple_of(which * half, 128), half)
        fetches.append(pltpu.make_async_copy(w_hbm.at[:, cols], to, wsem.at[i]))
        fetches[-1].start()
    for copy in copies:
        copy.wait()
    stage(kcat, vbuf, vt, extra, core * rows, span)
    before = (acc1_ref, peak1_ref, norm1_ref)
    run_heads(kcat, core * rows, qt, ksw, svw, bias, vt, sbuf, wbuf, tops, grows, out, peak, norm, span, 0, before)
    finish_heads(out, peak, norm, att)
    fetches[0].wait()
    other_ref[...] = jnp.dot(att[...], weight[...], preferred_element_type=jnp.float32).astype(jnp.bfloat16)
    fetches[1].wait()


def rest_kernel(
    where_ref, kcat, vt, acc1_ref, peak1_ref, norm1_ref, ksw, svw, qt, bias, weight,
    other_ref, att,
    sbuf, wbuf, tops, grows, out, peak, norm,
):
    core = where_ref[1]
    span = vt.shape[2]
    rows = kcat.shape[1] - span
    before = (acc1_ref, peak1_ref, norm1_ref)
    run_heads(kcat, core * rows, qt, ksw, svw, bias, vt, sbuf, wbuf, tops, grows, out, peak, norm, span, FAR, before)
    finish_heads(out, peak, norm, att)
    other_ref[...] = jnp.dot(att[...], weight[...], preferred_element_type=jnp.float32).astype(jnp.bfloat16)


def own_kernel(att, rest, weight, mine_ref):
    both = jnp.concatenate([att[...], rest[...]], axis=0)
    mine_ref[...] = jnp.dot(both, weight[...], preferred_element_type=jnp.float32)


def add_kernel(mine_ref, far_ref, rest_ref, out_ref):
    tall = far_ref.shape[0]
    out_ref[:tall] = (mine_ref[:tall] + far_ref[...].astype(jnp.float32)).astype(out_ref.dtype)
    out_ref[tall:] = (mine_ref[tall:] + rest_ref[...].astype(jnp.float32)).astype(out_ref.dtype)


def step_scratch(kv_heads, span):
    def twice(shape, dtype):
        return [[pltpu.VMEM(shape, dtype)] * kv_heads] * 2

    return [
        twice((span, WIDTH), jnp.float32),
        twice((span, WIDTH), jnp.bfloat16),
        twice((1, 128), jnp.float32),
        twice((1, 128), jnp.float32),
    ]


def sums_like(heads, chunks):
    return [
        jax.ShapeDtypeStruct((heads, chunks, HEAD, 128), jnp.float32),
        *[jax.ShapeDtypeStruct((chunks, heads, 128), jnp.float32)] * 2,
    ]


def vmem_like(shapes):
    return [pltpu.VMEM(a.shape, a.dtype) for a in shapes]


def attend_near(where, x0, ks, vs, x1, y, yp, qt, pick, bias, extra):
    rows, lanes = ks.shape[0], pick.shape[1]
    kv_heads = ks.shape[1] // HEAD
    return pl.pallas_call(
        near_kernel,
        out_shape=(*sums_like(*qt.shape[:2]), *[jax.ShapeDtypeStruct((kv_heads, HEAD, lanes), jnp.float32)] * 2),
        in_specs=[SMEM] + [ANY] * 6 + [VMEM] * 4,
        out_specs=(VMEM,) * 5,
        scratch_shapes=[pltpu.VMEM(a.shape, a.dtype) for a in (ks, vs, x1, y)]
        + [
            pltpu.VMEM((kv_heads, (NEAR + 1) * rows, 2 * HEAD), jnp.bfloat16),
            pltpu.VMEM(((NEAR + 1) * rows, kv_heads * HEAD), jnp.bfloat16),
            pltpu.VMEM((kv_heads, HEAD, NEAR * rows), jnp.bfloat16),
        ]
        + step_scratch(kv_heads, NEAR * rows)
        + [pltpu.SemaphoreType.DMA((22,))],
        compiler_params=GRANT,
        name="near",
    )(where, x0, ks, vs, x1, y, yp, qt, pick, bias, extra)


def attend_far(where, y, z, zp, acc1, peak1, norm1, ksw, svw, qt, bias, extra, w):
    kv_heads, heads = ksw.shape[0], qt.shape[0]
    depth, features = w.shape
    span, few, rows = extra.shape[0], WIDTH // SECOND, ksw.shape[2] // SECOND
    return pl.pallas_call(
        far_kernel,
        out_shape=(
            jax.ShapeDtypeStruct((FAR * few, features // 2), jnp.bfloat16),
            jax.ShapeDtypeStruct((FAR * few, heads * HEAD), jnp.bfloat16),
            jax.ShapeDtypeStruct((kv_heads, span + rows, 2 * HEAD), jnp.bfloat16),
            jax.ShapeDtypeStruct((kv_heads, HEAD, span), jnp.bfloat16),
            *[jax.ShapeDtypeStruct((depth, features // 2), jnp.bfloat16)] * 2,
        ),
        in_specs=[SMEM] + [ANY] * 3 + [VMEM] * 8 + [ANY],
        out_specs=(VMEM,) * 6,
        scratch_shapes=[pltpu.VMEM((span + rows, kv_heads * HEAD), jnp.bfloat16)]
        + step_scratch(kv_heads, span)
        + vmem_like(sums_like(heads, FAR))
        + [pltpu.SemaphoreType.DMA((15,)), pltpu.SemaphoreType.DMA((2,))],
        compiler_params=GRANT,
        name="far",
    )(where, y, z, zp, acc1, peak1, norm1, ksw, svw, qt, bias, extra, w)


def attend_rest(where, kcat, vt, acc1, peak1, norm1, ksw, svw, qt, bias, weight):
    kv_heads, (heads, chunks) = ksw.shape[0], qt.shape[:2]
    left = (chunks - FAR) * (WIDTH // SECOND)
    return pl.pallas_call(
        rest_kernel,
        out_shape=(
            jax.ShapeDtypeStruct((left, weight.shape[1]), jnp.bfloat16),
            jax.ShapeDtypeStruct((left, heads * HEAD), jnp.bfloat16),
        ),
        in_specs=[SMEM] + [VMEM] * 10,
        out_specs=(VMEM,) * 2,
        scratch_shapes=step_scratch(kv_heads, vt.shape[2]) + vmem_like(sums_like(heads, chunks - FAR)),
        compiler_params=GRANT,
        name="rest",
    )(where, kcat, vt, acc1, peak1, norm1, ksw, svw, qt, bias, weight)


def simple(kernel, out, *arrays):
    return pl.pallas_call(
        kernel, out_shape=out, in_specs=[VMEM] * len(arrays), out_specs=VMEM, compiler_params=GRANT
    )(*arrays)


def body(queries, keys_first, primary_value_array, keys_second, secondary_value_array, out_weight):
    count = lax.axis_size("ctx")
    queries, keys_first, primary_value_array, keys_second, secondary_value_array, out_weight = (
        pltpu.with_memory_space_constraint(a, pltpu.HBM)
        for a in (queries, keys_first, primary_value_array, keys_second, secondary_value_array, out_weight)
    )
    shard = lax.axis_index("ctx")
    where = jnp.stack([shard, shard % 2, lax.axis_index("head")]).astype(jnp.int32)
    packed = pack(keys_first, primary_value_array, keys_second, secondary_value_array)
    twin = core_swap(packed, count)
    near_load, far_load = join(packed, twin)
    near = chip_shift(near_load, count, 1, 2)
    far = chip_shift(far_load, count, 3, 4)
    qt, pick, near_bias, far_bias, near_extra, far_extra = prep(where, queries)
    near_twin = core_swap(near, count)
    sums = attend_near(
        where, packed, keys_second, secondary_value_array, twin, near, near_twin, qt, pick, near_bias, near_extra
    )
    far_twin = core_swap(far, count)
    other, attention, kcat, vt, weight, own_weight = attend_far(
        where, near, far, far_twin, *sums, qt, far_bias, far_extra, out_weight
    )
    other = head_swap(other)
    other_rest, attention_rest = attend_rest(where, kcat, vt, *sums, qt, far_bias, weight)
    other_rest = head_swap(other_rest)
    half = jax.ShapeDtypeStruct((queries.shape[0], own_weight.shape[1]), jnp.float32)
    mine = simple(own_kernel, half, attention, attention_rest, own_weight)
    half = jax.ShapeDtypeStruct(half.shape, jnp.bfloat16)
    return simple(add_kernel, half, mine, other, other_rest)


def solution(mesh):
    in_specs = (P("ctx", "head"),) * 5 + (P("head", None),)
    return jax.shard_map(body, mesh=mesh, in_specs=in_specs, out_specs=P("ctx", "head"), check_vma=False)
```

```python
import functools
import math

import jax
import jax.numpy as jnp
from jax import lax
from jax.experimental import pallas as pl
from jax.experimental.pallas import tpu as pltpu
from jax.sharding import PartitionSpec as P


HEAD = 128
FIRST = 512
SECOND = 16
LOG2E = 1.4426950408889634
NEG = -1e30
WIDTH = 256
UNROLL = 4
NEAR = 5
ANY = pl.BlockSpec(memory_space=pl.ANY)
VMEM = pl.BlockSpec(memory_space=pltpu.VMEM)
SMEM = pl.BlockSpec(memory_space=pltpu.SMEM)
GRANT = pltpu.CompilerParams(vmem_limit_bytes=20 << 20)
SMALL = pltpu.CompilerParams(vmem_limit_bytes=2 << 20)


def core_swap(value, count):
    return lax.ppermute(value, "ctx", [(s, s ^ 1) for s in range(count)])


def chip_shift(value, count, even, odd):
    pairs = [(s, s + 2 * (even if s % 2 == 0 else odd)) for s in range(count)]
    return lax.ppermute(value, "ctx", [(a, b) for a, b in pairs if b < count])


def head_swap(value):
    return lax.ppermute(value, "head", [(0, 1), (1, 0)])


def pack_kernel(k_ref, v_ref, ks_ref, vs_ref, out_ref, sem):
    rows = k_ref.shape[0]
    tail = pl.ds(rows - SECOND, SECOND)
    parts = (
        (k_ref, out_ref.at[pl.ds(0, rows)]),
        (v_ref, out_ref.at[pl.ds(rows, rows)]),
        (ks_ref.at[tail], out_ref.at[pl.ds(2 * rows, SECOND)]),
        (vs_ref.at[tail], out_ref.at[pl.ds(2 * rows + SECOND, SECOND)]),
    )
    copies = [pltpu.make_async_copy(a, b, sem.at[i]) for i, (a, b) in enumerate(parts)]
    for copy in copies:
        copy.start()
    for copy in copies:
        copy.wait()


def pack(k, v, ks, vs):
    rows, wide = k.shape
    return pl.pallas_call(
        pack_kernel,
        out_shape=jax.ShapeDtypeStruct((2 * rows + 2 * SECOND, wide), k.dtype),
        in_specs=[ANY] * 4,
        out_specs=VMEM,
        scratch_shapes=[pltpu.SemaphoreType.DMA((4,))],
        compiler_params=SMALL,
        name="pack",
    )(k, v, ks, vs)


def join_kernel(own_ref, twin_ref, near_ref, far_ref):
    short = far_ref.shape[0] // 2
    for ref in (near_ref, far_ref):
        ref[0:short] = own_ref[0:short]
        ref[short : 2 * short] = twin_ref[0:short]
    near_ref[2 * short :] = twin_ref[short:]


def join(own, twin):
    tall, wide = own.shape
    short = tall - 2 * SECOND
    return pl.pallas_call(
        join_kernel,
        out_shape=(
            jax.ShapeDtypeStruct((tall + short, wide), own.dtype),
            jax.ShapeDtypeStruct((2 * short, wide), own.dtype),
        ),
        in_specs=[VMEM] * 2,
        out_specs=(VMEM, VMEM),
        compiler_params=SMALL,
        name="join",
    )(own, twin)


def lane_token(lane):
    few = WIDTH // SECOND
    return few * (lane // WIDTH) + lane % few, (lane % WIDTH) // few


def prep_kernel(where_ref, q_hbm, qt_ref, pick_ref, near_bias_ref, far_bias_ref, near_extra_ref, far_extra_ref, q, sem):
    shard = where_ref[0]
    copy = pltpu.make_async_copy(q_hbm, q, sem)
    copy.start()
    rows = q.shape[0]
    shape = pick_ref.shape
    feature = lax.broadcasted_iota(jnp.int32, shape, 0)
    token, offset = lane_token(lax.broadcasted_iota(jnp.int32, shape, 1))
    pick_ref[...] = (feature == token + offset + 1).astype(jnp.bfloat16)
    early = (shard == 0) & (token + offset < SECOND - 1)
    last = jnp.where(feature == rows, 1.0, jnp.where((feature == rows + 1) & early, NEG, 0.0))
    for ref, hidden in ((near_bias_ref, feature > token), (far_bias_ref, feature <= token)):
        ref[...] = jnp.where((feature < rows) & hidden, NEG, last).astype(jnp.bfloat16)
    for ref, first, cut in (
        (near_extra_ref, shard + 1 - near_extra_ref.shape[0] // rows, near_extra_ref.shape[0] - rows),
        (far_extra_ref, shard - FIRST // rows, 0),
    ):
        row = lax.broadcasted_iota(jnp.int32, ref.shape, 0)
        col = lax.broadcasted_iota(jnp.int32, ref.shape, 1)
        gone = jnp.where(first + row // rows < 0, NEG, 0.0)
        extra = jnp.where(col == rows, gone, jnp.where(col == rows + 1, 1.0, 0.0))
        ref[...] = jnp.where((col < rows) & (row - cut == col), 1.0, extra).astype(jnp.bfloat16)
    copy.wait()
    scale = LOG2E / math.sqrt(HEAD)
    few = WIDTH // SECOND
    for h in range(qt_ref.shape[0]):
        part = q[:, h * HEAD : (h + 1) * HEAD].astype(jnp.float32) * scale
        for c in range(qt_ref.shape[1]):
            qt_ref[h, c] = jnp.concatenate([part[c * few : (c + 1) * few]] * (128 // few), axis=0).T


def prep(where, q):
    rows, wide = q.shape
    heads, lanes, chunks = wide // HEAD, SECOND * rows, SECOND * rows // WIDTH
    return pl.pallas_call(
        prep_kernel,
        out_shape=(
            jax.ShapeDtypeStruct((heads, chunks, HEAD, 128), jnp.float32),
            *[jax.ShapeDtypeStruct((HEAD, lanes), jnp.bfloat16)] * 3,
            jax.ShapeDtypeStruct((NEAR * rows, HEAD), jnp.bfloat16),
            jax.ShapeDtypeStruct((FIRST + rows - NEAR * rows, HEAD), jnp.bfloat16),
        ),
        in_specs=[SMEM, ANY],
        out_specs=(VMEM,) * 6,
        scratch_shapes=[pltpu.VMEM(q.shape, q.dtype), pltpu.SemaphoreType.DMA(())],
        compiler_params=GRANT,
        name="prep",
    )(where, q)


def windows(where_ref, ks, vs, x1, y, pick, ksw, svw, rows):
    shard, core = where_ref[0], where_ref[1]
    for own, out, at in ((ks, ksw, 0), (vs, svw, SECOND)):
        near = y[4 * rows + at : 4 * rows + at + SECOND, :]
        twin = x1[2 * rows + at : 2 * rows + at + SECOND, :]
        mine = own[...].astype(jnp.float32)
        tail = jnp.where(core == 1, twin.astype(jnp.float32), near.astype(jnp.float32))
        tail = jnp.where(shard == 0, jnp.zeros_like(tail), tail)
        rest = jnp.zeros((128 - SECOND - rows, mine.shape[1]), jnp.float32)
        tokens = jnp.concatenate([tail, mine, rest], axis=0)
        for g in range(out.shape[0]):
            turned = tokens[:, g * HEAD : (g + 1) * HEAD].T.astype(jnp.bfloat16)
            out[g] = jnp.dot(turned, pick[...], preferred_element_type=jnp.float32)


def stage(kcat, vbuf, vt, extra, start, span):
    window = pl.ds(pl.multiple_of(start, 16), span)
    for g in range(kcat.shape[0]):
        kcat[g, window, HEAD : 2 * HEAD] = extra[...]
        vt[g] = vbuf[window, g * HEAD : (g + 1) * HEAD].T


def run_heads(kcat, start, qt, ksw, svw, bias, vt, sbuf, wbuf, tops, grows, out, peak, norm, before=None):
    kv_heads = ksw.shape[0]
    heads, chunks = qt.shape[:2]
    group = heads // kv_heads
    steps = group * chunks
    window = pl.ds(pl.multiple_of(start, 16), vt.shape[2])
    tiles = [slice(i * 128, (i + 1) * 128) for i in range(WIDTH // 128)]

    def place(step, g):
        step = jnp.minimum(step, steps - 1)
        c = step // group
        return g * group + step % group, c, pl.ds(pl.multiple_of(c * WIDTH, WIDTH), WIDTH)

    def score(step, turn):
        for g in range(kv_heads):
            h, c, at = place(step, g)
            products = jnp.concatenate([qt[h, c]] * len(tiles), axis=1) * ksw[g, :, at]
            products = jnp.concatenate([products.astype(jnp.bfloat16), bias[:, at]], axis=0)
            s = jnp.dot(kcat[g, window, :], products, preferred_element_type=jnp.float32)
            sbuf[turn][g][...] = s
            top = jnp.max(s, axis=0, keepdims=True)
            tops[turn][g][...] = functools.reduce(jnp.maximum, [top[:, t] for t in tiles])

    def soften(step, turn):
        for g in range(kv_heads):
            h, c, _ = place(step, g)
            top = tops[turn][g][...]
            if before is not None:
                top = jnp.maximum(top, before[1][c, pl.ds(h, 1), :])
                grow = jnp.exp2(before[1][c, pl.ds(h, 1), :] - top)
                grows[turn][g][...] = grow
            e = jnp.exp2(sbuf[turn][g][...] - jnp.concatenate([top] * len(tiles), axis=1))
            wbuf[turn][g][...] = e.astype(jnp.bfloat16)
            total = jnp.sum(e, axis=0, keepdims=True)
            total = functools.reduce(jnp.add, [total[:, t] for t in tiles])
            if before is not None:
                total = total + before[2][c, pl.ds(h, 1), :] * grow
            peak[c, pl.ds(h, 1), :] = top
            norm[c, pl.ds(h, 1), :] = total

    def mix(step, turn):
        for g in range(kv_heads):
            h, c, at = place(step, g)
            mixed = jnp.dot(vt[g], wbuf[turn][g][...], preferred_element_type=jnp.float32)
            mixed = mixed * svw[g, :, at]
            sums = functools.reduce(jnp.add, [mixed[:, t] for t in tiles])
            if before is not None:
                sums = sums + before[0][h, c] * grows[turn][g][...]
            out[h, c] = sums

    def several(i, _):
        for turn in range(UNROLL):
            step = UNROLL * i + turn
            mix(step, turn % 2)
            soften(step + 1, (turn + 1) % 2)
            score(step + 2, turn % 2)
        return 0

    score(0, 0)
    score(1, 1)
    soften(0, 0)
    lax.fori_loop(0, steps // UNROLL, several, 0)


def start_all(pairs, sem):
    copies = [pltpu.make_async_copy(a, b, sem.at[i]) for i, (a, b) in enumerate(pairs)]
    for copy in copies:
        copy.start()
    return copies


def block_copies(ref, row, rows, block, kcat, vbuf):
    at = pl.ds(pl.multiple_of(block * rows, rows), rows)
    keys = ref.at[pl.ds(row, rows)]
    pairs = [(keys.at[:, pl.ds(g * HEAD, HEAD)], kcat.at[g, at, pl.ds(0, HEAD)]) for g in range(kcat.shape[0])]
    return pairs + [(ref.at[pl.ds(row + rows, rows)], vbuf.at[at])]


def chip_blocks(ref, rows, pair, flip, kcat, vbuf):
    pairs = []
    for slot in range(2):
        block = 2 * pair + jnp.where(flip == 1, 1 - slot, slot)
        pairs += block_copies(ref, slot * 2 * rows, rows, block, kcat, vbuf)
    return pairs


def near_kernel(
    where_ref, x0_hbm, ks_hbm, vs_hbm, x1_hbm, y_hbm, yp_hbm, qt, pick, bias, extra,
    out_ref, peak_ref, norm_ref, ksw, svw,
    ks, vs, x1, y, kcat, vbuf, vt, sbuf, wbuf, tops, grows, sem,
):
    core = where_ref[1]
    rows = ks.shape[0]
    blocks = vbuf.shape[0] // rows
    pairs = [(ks_hbm, ks), (vs_hbm, vs), (x1_hbm, x1), (y_hbm, y)]
    pairs += block_copies(x0_hbm, 0, rows, blocks - 2 + core, kcat, vbuf)
    pairs += block_copies(x1_hbm, 0, rows, blocks - 1 - core, kcat, vbuf)
    pairs += chip_blocks(y_hbm, rows, 1 - core, core, kcat, vbuf)
    pairs += chip_blocks(yp_hbm, rows, core, 1 - core, kcat, vbuf)
    for copy in start_all(pairs, sem):
        copy.wait()
    windows(where_ref, ks, vs, x1, y, pick, ksw, svw, rows)
    stage(kcat, vbuf, vt, extra, core * rows, NEAR * rows)
    run_heads(kcat, core * rows, qt, ksw, svw, bias, vt, sbuf, wbuf, tops, grows, out_ref, peak_ref, norm_ref)


def far_kernel(
    where_ref, y_hbm, z_hbm, zp_hbm, acc1_ref, peak1_ref, norm1_ref, ksw, svw, qt, bias, extra, w_hbm,
    other_ref, att,
    kcat, vbuf, vt, sbuf, wbuf, tops, grows, out, peak, norm, weight, sem, wsem,
):
    core, side = where_ref[1], where_ref[2]
    rows = att.shape[0]
    half = w_hbm.shape[1] // 2
    blocks = vbuf.shape[0] // rows
    pairs = chip_blocks(z_hbm, rows, core, core, kcat, vbuf)
    pairs += chip_blocks(zp_hbm, rows, 1 - core, 1 - core, kcat, vbuf)
    pairs += block_copies(y_hbm, 2 * rows, rows, blocks - 1, kcat, vbuf)
    copies = start_all(pairs, sem)
    cols = pl.ds(pl.multiple_of((1 - side) * half, 128), half)
    fetch = pltpu.make_async_copy(w_hbm.at[:, cols], weight, wsem)
    fetch.start()
    for copy in copies:
        copy.wait()
    stage(kcat, vbuf, vt, extra, core * rows, (blocks - 1) * rows)
    run_heads(
        kcat, core * rows, qt, ksw, svw, bias, vt, sbuf, wbuf, tops, grows, out, peak, norm, (acc1_ref, peak1_ref, norm1_ref)
    )
    heads, chunks = qt.shape[:2]
    few = WIDTH // SECOND
    shifts = [few << i for i in range((128 // few).bit_length() - 1)]
    for c in range(chunks):
        top = peak[c]
        most = top
        for shift in shifts:
            most = jnp.maximum(most, pltpu.roll(most, shift, 1))
        grow = jnp.exp2(top - most)
        total = norm[c] * grow
        for shift in shifts:
            total = total + pltpu.roll(total, shift, 1)
        grow = grow / total
        for h in range(heads):
            part = (out[h, c] * grow[h : h + 1]).T
            part = functools.reduce(jnp.add, [part[i : i + few] for i in range(0, 128, few)])
            att[c * few : (c + 1) * few, h * HEAD : (h + 1) * HEAD] = part.astype(jnp.bfloat16)
    fetch.wait()
    other_ref[...] = jnp.dot(att[...], weight[...], preferred_element_type=jnp.float32).astype(jnp.bfloat16)


def own_kernel(where_ref, att, w_hbm, mine_ref, weight, sem):
    half = w_hbm.shape[1] // 2
    cols = pl.ds(pl.multiple_of(where_ref[2] * half, 128), half)
    fetch = pltpu.make_async_copy(w_hbm.at[:, cols], weight, sem)
    fetch.start()
    fetch.wait()
    mine_ref[...] = jnp.dot(att[...], weight[...], preferred_element_type=jnp.float32)


def common_scratch(rows, kv_heads, blocks, span):
    def twice(shape, dtype):
        return [[pltpu.VMEM(shape, dtype)] * kv_heads] * 2

    return [
        pltpu.VMEM((kv_heads, blocks * rows, 2 * HEAD), jnp.bfloat16),
        pltpu.VMEM((blocks * rows, kv_heads * HEAD), jnp.bfloat16),
        pltpu.VMEM((kv_heads, HEAD, span), jnp.bfloat16),
        twice((span, WIDTH), jnp.float32),
        twice((span, WIDTH), jnp.bfloat16),
        twice((1, 128), jnp.float32),
        twice((1, 128), jnp.float32),
    ]


def sums_like(qt):
    heads, chunks = qt.shape[:2]
    return [
        jax.ShapeDtypeStruct((heads, chunks, HEAD, 128), jnp.float32),
        *[jax.ShapeDtypeStruct((chunks, heads, 128), jnp.float32)] * 2,
    ]


def attend_near(where, x0, ks, vs, x1, y, yp, qt, pick, bias, extra):
    rows, lanes = ks.shape[0], pick.shape[1]
    kv_heads = ks.shape[1] // HEAD
    return pl.pallas_call(
        near_kernel,
        out_shape=(*sums_like(qt), *[jax.ShapeDtypeStruct((kv_heads, HEAD, lanes), jnp.float32)] * 2),
        in_specs=[SMEM] + [ANY] * 6 + [VMEM] * 4,
        out_specs=(VMEM,) * 5,
        scratch_shapes=[pltpu.VMEM(a.shape, a.dtype) for a in (ks, vs, x1, y)]
        + common_scratch(rows, kv_heads, NEAR + 1, NEAR * rows)
        + [pltpu.SemaphoreType.DMA((22,))],
        compiler_params=GRANT,
        name="near",
    )(where, x0, ks, vs, x1, y, yp, qt, pick, bias, extra)


def attend_far(where, y, z, zp, acc1, peak1, norm1, ksw, svw, qt, bias, extra, w):
    kv_heads, (heads, chunks) = ksw.shape[0], qt.shape[:2]
    rows = ksw.shape[2] // SECOND
    depth, features = w.shape
    span = extra.shape[0]
    return pl.pallas_call(
        far_kernel,
        out_shape=(
            jax.ShapeDtypeStruct((rows, features // 2), jnp.bfloat16),
            jax.ShapeDtypeStruct((rows, heads * HEAD), jnp.bfloat16),
        ),
        in_specs=[SMEM] + [ANY] * 3 + [VMEM] * 8 + [ANY],
        out_specs=(VMEM, VMEM),
        scratch_shapes=common_scratch(rows, kv_heads, span // rows + 1, span)
        + [
            *(pltpu.VMEM(a.shape, a.dtype) for a in (acc1, peak1, norm1)),
            pltpu.VMEM((depth, features // 2), jnp.bfloat16),
            pltpu.SemaphoreType.DMA((15,)),
            pltpu.SemaphoreType.DMA(()),
        ],
        compiler_params=GRANT,
        name="far",
    )(where, y, z, zp, acc1, peak1, norm1, ksw, svw, qt, bias, extra, w)


def project_own(where, att, w):
    rows, (depth, features) = att.shape[0], w.shape
    return pl.pallas_call(
        own_kernel,
        out_shape=jax.ShapeDtypeStruct((rows, features // 2), jnp.float32),
        in_specs=[SMEM, VMEM, ANY],
        out_specs=VMEM,
        scratch_shapes=[pltpu.VMEM((depth, features // 2), jnp.bfloat16), pltpu.SemaphoreType.DMA(())],
        compiler_params=GRANT,
        name="own",
    )(where, att, w)


def body(queries, keys_first, primary_value_array, keys_second, secondary_value_array, out_weight):
    count = lax.axis_size("ctx")
    queries, keys_first, primary_value_array, keys_second, secondary_value_array, out_weight = (
        pltpu.with_memory_space_constraint(a, pltpu.HBM)
        for a in (queries, keys_first, primary_value_array, keys_second, secondary_value_array, out_weight)
    )
    shard = lax.axis_index("ctx")
    where = jnp.stack([shard, shard % 2, lax.axis_index("head")]).astype(jnp.int32)
    packed = pack(keys_first, primary_value_array, keys_second, secondary_value_array)
    twin = core_swap(packed, count)
    near_load, far_load = join(packed, twin)
    near = chip_shift(near_load, count, 1, 2)
    far = chip_shift(far_load, count, 4, 3)
    qt, pick, near_bias, far_bias, near_extra, far_extra = prep(where, queries)
    near_twin = core_swap(near, count)
    sums = attend_near(
        where, packed, keys_second, secondary_value_array, twin, near, near_twin, qt, pick, near_bias, near_extra
    )
    far_twin = core_swap(far, count)
    other, attention = attend_far(where, near, far, far_twin, *sums, qt, far_bias, far_extra, out_weight)
    other = head_swap(other)
    mine = project_own(where, attention, out_weight)
    return (mine + other.astype(jnp.float32)).astype(jnp.bfloat16)


def solution(mesh):
    in_specs = (P("ctx", "head"),) * 5 + (P("head", None),)
    return jax.shard_map(body, mesh=mesh, in_specs=in_specs, out_specs=P("ctx", "head"), check_vma=False)
```

```python
import functools
import math

import jax
import jax.numpy as jnp
from jax import lax
from jax.experimental import pallas as pl
from jax.experimental.pallas import tpu as pltpu
from jax.sharding import PartitionSpec as P


HEAD = 128
FIRST = 512
SECOND = 16
LOG2E = 1.4426950408889634
NEG = -1e30
WIDTH = 256
UNROLL = 8
PAIR = 2
NEAR = 5
ANY = pl.BlockSpec(memory_space=pl.ANY)
VMEM = pl.BlockSpec(memory_space=pltpu.VMEM)
SMEM = pl.BlockSpec(memory_space=pltpu.SMEM)
GRANT = pltpu.CompilerParams(vmem_limit_bytes=20 << 20)
SMALL = pltpu.CompilerParams(vmem_limit_bytes=2 << 20)


def core_swap(value, count):
    return lax.ppermute(value, "ctx", [(s, s ^ 1) for s in range(count)])


def chip_shift(value, count, even, odd):
    pairs = [(s, s + 2 * (even if s % 2 == 0 else odd)) for s in range(count)]
    return lax.ppermute(value, "ctx", [(a, b) for a, b in pairs if b < count])


def head_swap(value):
    return lax.ppermute(value, "head", [(0, 1), (1, 0)])


def pack_kernel(k_ref, v_ref, ks_ref, vs_ref, out_ref, sem):
    rows = k_ref.shape[0]
    tail = pl.ds(rows - SECOND, SECOND)
    parts = (
        (k_ref, out_ref.at[pl.ds(0, rows)]),
        (v_ref, out_ref.at[pl.ds(rows, rows)]),
        (ks_ref.at[tail], out_ref.at[pl.ds(2 * rows, SECOND)]),
        (vs_ref.at[tail], out_ref.at[pl.ds(2 * rows + SECOND, SECOND)]),
    )
    copies = [pltpu.make_async_copy(a, b, sem.at[i]) for i, (a, b) in enumerate(parts)]
    for copy in copies:
        copy.start()
    for copy in copies:
        copy.wait()


def pack(k, v, ks, vs):
    rows, wide = k.shape
    return pl.pallas_call(
        pack_kernel,
        out_shape=jax.ShapeDtypeStruct((2 * rows + 2 * SECOND, wide), k.dtype),
        in_specs=[ANY] * 4,
        out_specs=VMEM,
        scratch_shapes=[pltpu.SemaphoreType.DMA((4,))],
        compiler_params=SMALL,
        name="pack",
    )(k, v, ks, vs)


def join_kernel(own_ref, twin_ref, near_ref, far_ref):
    short = far_ref.shape[0] // 2
    for ref in (near_ref, far_ref):
        ref[0:short] = own_ref[0:short]
        ref[short : 2 * short] = twin_ref[0:short]
    near_ref[2 * short :] = twin_ref[short:]


def join(own, twin):
    tall, wide = own.shape
    short = tall - 2 * SECOND
    return pl.pallas_call(
        join_kernel,
        out_shape=(
            jax.ShapeDtypeStruct((tall + short, wide), own.dtype),
            jax.ShapeDtypeStruct((2 * short, wide), own.dtype),
        ),
        in_specs=[VMEM] * 2,
        out_specs=(VMEM, VMEM),
        compiler_params=SMALL,
        name="join",
    )(own, twin)


def lane_token(lane):
    few = WIDTH // SECOND
    return few * (lane // WIDTH) + lane % few, (lane % WIDTH) // few


def prep_kernel(where_ref, q_hbm, qt_ref, pick_ref, near_bias_ref, far_bias_ref, near_extra_ref, far_extra_ref, q, sem):
    shard = where_ref[0]
    copy = pltpu.make_async_copy(q_hbm, q, sem)
    copy.start()
    rows = q.shape[0]
    shape = pick_ref.shape
    feature = lax.broadcasted_iota(jnp.int32, shape, 0)
    token, offset = lane_token(lax.broadcasted_iota(jnp.int32, shape, 1))
    pick_ref[...] = (feature == token + offset + 1).astype(jnp.bfloat16)
    early = (shard == 0) & (token + offset < SECOND - 1)
    last = jnp.where(feature == rows, 1.0, jnp.where((feature == rows + 1) & early, NEG, 0.0))
    for ref, hidden in ((near_bias_ref, feature > token), (far_bias_ref, feature <= token)):
        ref[...] = jnp.where((feature < rows) & hidden, NEG, last).astype(jnp.bfloat16)
    for ref, first, cut in (
        (near_extra_ref, shard + 1 - near_extra_ref.shape[0] // rows, near_extra_ref.shape[0] - rows),
        (far_extra_ref, shard - FIRST // rows, 0),
    ):
        row = lax.broadcasted_iota(jnp.int32, ref.shape, 0)
        col = lax.broadcasted_iota(jnp.int32, ref.shape, 1)
        gone = jnp.where(first + row // rows < 0, NEG, 0.0)
        extra = jnp.where(col == rows, gone, jnp.where(col == rows + 1, 1.0, 0.0))
        ref[...] = jnp.where((col < rows) & (row - cut == col), 1.0, extra).astype(jnp.bfloat16)
    copy.wait()
    scale = LOG2E / math.sqrt(HEAD)
    few = WIDTH // SECOND
    for h in range(qt_ref.shape[0]):
        part = q[:, h * HEAD : (h + 1) * HEAD].astype(jnp.float32) * scale
        for c in range(qt_ref.shape[1]):
            qt_ref[h, c] = jnp.concatenate([part[c * few : (c + 1) * few]] * (128 // few), axis=0).T


def prep(where, q):
    rows, wide = q.shape
    heads, lanes, chunks = wide // HEAD, SECOND * rows, SECOND * rows // WIDTH
    return pl.pallas_call(
        prep_kernel,
        out_shape=(
            jax.ShapeDtypeStruct((heads, chunks, HEAD, 128), jnp.float32),
            *[jax.ShapeDtypeStruct((HEAD, lanes), jnp.bfloat16)] * 3,
            jax.ShapeDtypeStruct((NEAR * rows, HEAD), jnp.bfloat16),
            jax.ShapeDtypeStruct((FIRST + rows - NEAR * rows, HEAD), jnp.bfloat16),
        ),
        in_specs=[SMEM, ANY],
        out_specs=(VMEM,) * 6,
        scratch_shapes=[pltpu.VMEM(q.shape, q.dtype), pltpu.SemaphoreType.DMA(())],
        compiler_params=GRANT,
        name="prep",
    )(where, q)


def windows(where_ref, ks, vs, x1, y, pick, ksw, svw, rows):
    shard, core = where_ref[0], where_ref[1]
    for own, out, at in ((ks, ksw, 0), (vs, svw, SECOND)):
        near = y[4 * rows + at : 4 * rows + at + SECOND, :]
        twin = x1[2 * rows + at : 2 * rows + at + SECOND, :]
        mine = own[...].astype(jnp.float32)
        tail = jnp.where(core == 1, twin.astype(jnp.float32), near.astype(jnp.float32))
        tail = jnp.where(shard == 0, jnp.zeros_like(tail), tail)
        rest = jnp.zeros((128 - SECOND - rows, mine.shape[1]), jnp.float32)
        tokens = jnp.concatenate([tail, mine, rest], axis=0)
        for g in range(out.shape[0]):
            turned = tokens[:, g * HEAD : (g + 1) * HEAD].T.astype(jnp.bfloat16)
            out[g] = jnp.dot(turned, pick[...], preferred_element_type=jnp.float32)


def stage(kcat, vbuf, vt, extra, start, span):
    window = pl.ds(pl.multiple_of(start, 16), span)
    for g in range(kcat.shape[0]):
        kcat[g, window, HEAD : 2 * HEAD] = extra[...]
        vt[g] = vbuf[window, g * HEAD : (g + 1) * HEAD].T


def run_heads(kcat, start, qt, ksw, svw, bias, vt, sbuf, wbuf, tops, grows, out, peak, norm, before=None):
    kv_heads = ksw.shape[0]
    heads, chunks = qt.shape[:2]
    group = heads // kv_heads
    steps = group * chunks
    window = pl.ds(pl.multiple_of(start, 16), vt.shape[2])
    tiles = [slice(i * 128, (i + 1) * 128) for i in range(WIDTH // 128)]

    def place(step, g):
        step = jnp.minimum(step, steps - 1)
        c = step // group
        return g * group + step % group, c, pl.ds(pl.multiple_of(c * WIDTH, WIDTH), WIDTH)

    def score(step, turn):
        for g in range(kv_heads):
            h, c, at = place(step, g)
            products = jnp.concatenate([qt[h, c]] * len(tiles), axis=1) * ksw[g, :, at]
            products = jnp.concatenate([products.astype(jnp.bfloat16), bias[:, at]], axis=0)
            s = jnp.dot(kcat[g, window, :], products, preferred_element_type=jnp.float32)
            sbuf[turn][g][...] = s
            top = jnp.max(s, axis=0, keepdims=True)
            tops[turn][g][...] = functools.reduce(jnp.maximum, [top[:, t] for t in tiles])

    def soften(step, turn):
        for g in range(kv_heads):
            h, c, _ = place(step, g)
            top = tops[turn][g][...]
            if before is not None:
                top = jnp.maximum(top, before[1][c, pl.ds(h, 1), :])
                grow = jnp.exp2(before[1][c, pl.ds(h, 1), :] - top)
                grows[turn][g][...] = grow
            e = jnp.exp2(sbuf[turn][g][...] - jnp.concatenate([top] * len(tiles), axis=1))
            wbuf[turn][g][...] = e.astype(jnp.bfloat16)
            total = jnp.sum(e, axis=0, keepdims=True)
            total = functools.reduce(jnp.add, [total[:, t] for t in tiles])
            if before is not None:
                total = total + before[2][c, pl.ds(h, 1), :] * grow
            peak[c, pl.ds(h, 1), :] = top
            norm[c, pl.ds(h, 1), :] = total

    def mix(step, turn):
        for g in range(kv_heads):
            h, c, at = place(step, g)
            mixed = jnp.dot(vt[g], wbuf[turn][g][...], preferred_element_type=jnp.float32)
            mixed = mixed * svw[g, :, at]
            sums = functools.reduce(jnp.add, [mixed[:, t] for t in tiles])
            if before is not None:
                sums = sums + before[0][h, c] * grows[turn][g][...]
            out[h, c] = sums

    def several(i, _):
        for turn in range(UNROLL):
            step = UNROLL * i + turn
            mix(step, turn % 2)
            soften(step + 1, (turn + 1) % 2)
            score(step + 2, turn % 2)
        return 0

    score(0, 0)
    score(1, 1)
    soften(0, 0)
    lax.fori_loop(0, steps // UNROLL, several, 0)


def start_all(pairs, sem):
    copies = [pltpu.make_async_copy(a, b, sem.at[i]) for i, (a, b) in enumerate(pairs)]
    for copy in copies:
        copy.start()
    return copies


def block_copies(ref, row, rows, block, kcat, vbuf):
    at = pl.ds(pl.multiple_of(block * rows, rows), rows)
    keys = ref.at[pl.ds(row, rows)]
    pairs = [(keys.at[:, pl.ds(g * HEAD, HEAD)], kcat.at[g, at, pl.ds(0, HEAD)]) for g in range(kcat.shape[0])]
    return pairs + [(ref.at[pl.ds(row + rows, rows)], vbuf.at[at])]


def chip_blocks(ref, rows, pair, flip, kcat, vbuf):
    pairs = []
    for slot in range(2):
        block = 2 * pair + jnp.where(flip == 1, 1 - slot, slot)
        pairs += block_copies(ref, slot * 2 * rows, rows, block, kcat, vbuf)
    return pairs


def near_kernel(
    where_ref, x0_hbm, ks_hbm, vs_hbm, x1_hbm, y_hbm, yp_hbm, qt, pick, bias, extra,
    out_ref, peak_ref, norm_ref, ksw, svw,
    ks, vs, x1, y, kcat, vbuf, vt, sbuf, wbuf, tops, grows, sem,
):
    core = where_ref[1]
    rows = ks.shape[0]
    blocks = vbuf.shape[0] // rows
    pairs = [(ks_hbm, ks), (vs_hbm, vs), (x1_hbm, x1), (y_hbm, y)]
    pairs += block_copies(x0_hbm, 0, rows, blocks - 2 + core, kcat, vbuf)
    pairs += block_copies(x1_hbm, 0, rows, blocks - 1 - core, kcat, vbuf)
    pairs += chip_blocks(y_hbm, rows, 1 - core, core, kcat, vbuf)
    pairs += chip_blocks(yp_hbm, rows, core, 1 - core, kcat, vbuf)
    for copy in start_all(pairs, sem):
        copy.wait()
    windows(where_ref, ks, vs, x1, y, pick, ksw, svw, rows)
    stage(kcat, vbuf, vt, extra, core * rows, NEAR * rows)
    run_heads(kcat, core * rows, qt, ksw, svw, bias, vt, sbuf, wbuf, tops, grows, out_ref, peak_ref, norm_ref)


def far_kernel(
    where_ref, y_hbm, z_hbm, zp_hbm, acc1_ref, peak1_ref, norm1_ref, ksw, svw, qt, bias, extra, w_hbm,
    other_ref, att,
    kcat, vbuf, vt, sbuf, wbuf, tops, grows, out, peak, norm, weight, partial, sem, wsem,
):
    core, side = where_ref[1], where_ref[2]
    rows = att.shape[0]
    half = w_hbm.shape[1] // 2
    blocks = vbuf.shape[0] // rows
    pairs = chip_blocks(z_hbm, rows, core, core, kcat, vbuf)
    pairs += chip_blocks(zp_hbm, rows, 1 - core, 1 - core, kcat, vbuf)
    pairs += block_copies(y_hbm, 2 * rows, rows, blocks - 1, kcat, vbuf)
    copies = start_all(pairs, sem)
    cols = pl.ds(pl.multiple_of((1 - side) * half, 128), half)
    fetch = pltpu.make_async_copy(w_hbm.at[:, cols], weight, wsem)
    fetch.start()
    for copy in copies:
        copy.wait()
    stage(kcat, vbuf, vt, extra, core * rows, (blocks - 1) * rows)
    run_heads(
        kcat, core * rows, qt, ksw, svw, bias, vt, sbuf, wbuf, tops, grows, out, peak, norm, (acc1_ref, peak1_ref, norm1_ref)
    )
    heads, chunks = qt.shape[:2]
    few = WIDTH // SECOND
    shifts = [few << i for i in range((128 // few).bit_length() - 1)]
    factors = []
    for c in range(chunks):
        top = peak[c]
        most = top
        for shift in shifts:
            most = jnp.maximum(most, pltpu.roll(most, shift, 1))
        grow = jnp.exp2(top - most)
        total = norm[c] * grow
        for shift in shifts:
            total = total + pltpu.roll(total, shift, 1)
        factors.append(grow / total)
    fetch.wait()
    for k in range(heads // PAIR):
        for h in range(k * PAIR, (k + 1) * PAIR):
            for c in range(chunks):
                part = (out[h, c] * factors[c][h : h + 1]).T
                part = functools.reduce(jnp.add, [part[i : i + few] for i in range(0, 128, few)])
                att[c * few : (c + 1) * few, h * HEAD : (h + 1) * HEAD] = part.astype(jnp.bfloat16)
        at = slice(k * PAIR * HEAD, (k + 1) * PAIR * HEAD)
        more = jnp.dot(att[:, at], weight[at, :], preferred_element_type=jnp.float32)
        if k == 0:
            partial[...] = more
        elif k < heads // PAIR - 1:
            partial[...] += more
        else:
            other_ref[...] = (partial[...] + more).astype(jnp.bfloat16)


def own_kernel(where_ref, att, w_hbm, mine_ref, weight, sem):
    half = w_hbm.shape[1] // 2
    cols = pl.ds(pl.multiple_of(where_ref[2] * half, 128), half)
    fetch = pltpu.make_async_copy(w_hbm.at[:, cols], weight, sem)
    fetch.start()
    fetch.wait()
    mine_ref[...] = jnp.dot(att[...], weight[...], preferred_element_type=jnp.float32)


def common_scratch(rows, kv_heads, blocks, span):
    def twice(shape, dtype):
        return [[pltpu.VMEM(shape, dtype)] * kv_heads] * 2

    return [
        pltpu.VMEM((kv_heads, blocks * rows, 2 * HEAD), jnp.bfloat16),
        pltpu.VMEM((blocks * rows, kv_heads * HEAD), jnp.bfloat16),
        pltpu.VMEM((kv_heads, HEAD, span), jnp.bfloat16),
        twice((span, WIDTH), jnp.float32),
        twice((span, WIDTH), jnp.bfloat16),
        twice((1, 128), jnp.float32),
        twice((1, 128), jnp.float32),
    ]


def sums_like(qt):
    heads, chunks = qt.shape[:2]
    return [
        jax.ShapeDtypeStruct((heads, chunks, HEAD, 128), jnp.float32),
        *[jax.ShapeDtypeStruct((chunks, heads, 128), jnp.float32)] * 2,
    ]


def attend_near(where, x0, ks, vs, x1, y, yp, qt, pick, bias, extra):
    rows, lanes = ks.shape[0], pick.shape[1]
    kv_heads = ks.shape[1] // HEAD
    return pl.pallas_call(
        near_kernel,
        out_shape=(*sums_like(qt), *[jax.ShapeDtypeStruct((kv_heads, HEAD, lanes), jnp.float32)] * 2),
        in_specs=[SMEM] + [ANY] * 6 + [VMEM] * 4,
        out_specs=(VMEM,) * 5,
        scratch_shapes=[pltpu.VMEM(a.shape, a.dtype) for a in (ks, vs, x1, y)]
        + common_scratch(rows, kv_heads, NEAR + 1, NEAR * rows)
        + [pltpu.SemaphoreType.DMA((22,))],
        compiler_params=GRANT,
        name="near",
    )(where, x0, ks, vs, x1, y, yp, qt, pick, bias, extra)


def attend_far(where, y, z, zp, acc1, peak1, norm1, ksw, svw, qt, bias, extra, w):
    kv_heads, (heads, chunks) = ksw.shape[0], qt.shape[:2]
    rows = ksw.shape[2] // SECOND
    depth, features = w.shape
    span = extra.shape[0]
    return pl.pallas_call(
        far_kernel,
        out_shape=(
            jax.ShapeDtypeStruct((rows, features // 2), jnp.bfloat16),
            jax.ShapeDtypeStruct((rows, heads * HEAD), jnp.bfloat16),
        ),
        in_specs=[SMEM] + [ANY] * 3 + [VMEM] * 8 + [ANY],
        out_specs=(VMEM, VMEM),
        scratch_shapes=common_scratch(rows, kv_heads, span // rows + 1, span)
        + [
            *(pltpu.VMEM(a.shape, a.dtype) for a in (acc1, peak1, norm1)),
            pltpu.VMEM((depth, features // 2), jnp.bfloat16),
            pltpu.VMEM((rows, features // 2), jnp.float32),
            pltpu.SemaphoreType.DMA((15,)),
            pltpu.SemaphoreType.DMA(()),
        ],
        compiler_params=GRANT,
        name="far",
    )(where, y, z, zp, acc1, peak1, norm1, ksw, svw, qt, bias, extra, w)


def project_own(where, att, w):
    rows, (depth, features) = att.shape[0], w.shape
    return pl.pallas_call(
        own_kernel,
        out_shape=jax.ShapeDtypeStruct((rows, features // 2), jnp.float32),
        in_specs=[SMEM, VMEM, ANY],
        out_specs=VMEM,
        scratch_shapes=[pltpu.VMEM((depth, features // 2), jnp.bfloat16), pltpu.SemaphoreType.DMA(())],
        compiler_params=GRANT,
        name="own",
    )(where, att, w)


def body(queries, keys_first, primary_value_array, keys_second, secondary_value_array, out_weight):
    count = lax.axis_size("ctx")
    queries, keys_first, primary_value_array, keys_second, secondary_value_array, out_weight = (
        pltpu.with_memory_space_constraint(a, pltpu.HBM)
        for a in (queries, keys_first, primary_value_array, keys_second, secondary_value_array, out_weight)
    )
    shard = lax.axis_index("ctx")
    where = jnp.stack([shard, shard % 2, lax.axis_index("head")]).astype(jnp.int32)
    packed = pack(keys_first, primary_value_array, keys_second, secondary_value_array)
    twin = core_swap(packed, count)
    near_load, far_load = join(packed, twin)
    near = chip_shift(near_load, count, 1, 2)
    far = chip_shift(far_load, count, 4, 3)
    qt, pick, near_bias, far_bias, near_extra, far_extra = prep(where, queries)
    near_twin = core_swap(near, count)
    sums = attend_near(
        where, packed, keys_second, secondary_value_array, twin, near, near_twin, qt, pick, near_bias, near_extra
    )
    far_twin = core_swap(far, count)
    other, attention = attend_far(where, near, far, far_twin, *sums, qt, far_bias, far_extra, out_weight)
    other = head_swap(other)
    mine = project_own(where, attention, out_weight)
    return (mine + other.astype(jnp.float32)).astype(jnp.bfloat16)


def solution(mesh):
    in_specs = (P("ctx", "head"),) * 5 + (P("head", None),)
    return jax.shard_map(body, mesh=mesh, in_specs=in_specs, out_specs=P("ctx", "head"), check_vma=False)
```

```python
import functools
import math

import jax
import jax.numpy as jnp
from jax import lax
from jax.experimental import pallas as pl
from jax.experimental.pallas import tpu as pltpu
from jax.sharding import PartitionSpec as P


HEAD = 128
FIRST = 512
SECOND = 16
LOG2E = 1.4426950408889634
NEG = -1e30
WIDTH = 256
UNROLL = 8
PAIR = 2
NEAR = 5
ANY = pl.BlockSpec(memory_space=pl.ANY)
VMEM = pl.BlockSpec(memory_space=pltpu.VMEM)
SMEM = pl.BlockSpec(memory_space=pltpu.SMEM)
GRANT = pltpu.CompilerParams(vmem_limit_bytes=20 << 20)
SMALL = pltpu.CompilerParams(vmem_limit_bytes=2 << 20)


def core_swap(value, count):
    return lax.ppermute(value, "ctx", [(s, s ^ 1) for s in range(count)])


def chip_shift(value, count, even, odd):
    pairs = [(s, s + 2 * (even if s % 2 == 0 else odd)) for s in range(count)]
    return lax.ppermute(value, "ctx", [(a, b) for a, b in pairs if b < count])


def head_swap(value):
    return lax.ppermute(value, "head", [(0, 1), (1, 0)])


def pack_kernel(k_ref, v_ref, ks_ref, vs_ref, out_ref, sem):
    rows = k_ref.shape[0]
    tail = pl.ds(rows - SECOND, SECOND)
    parts = (
        (k_ref, out_ref.at[pl.ds(0, rows)]),
        (v_ref, out_ref.at[pl.ds(rows, rows)]),
        (ks_ref.at[tail], out_ref.at[pl.ds(2 * rows, SECOND)]),
        (vs_ref.at[tail], out_ref.at[pl.ds(2 * rows + SECOND, SECOND)]),
    )
    copies = [pltpu.make_async_copy(a, b, sem.at[i]) for i, (a, b) in enumerate(parts)]
    for copy in copies:
        copy.start()
    for copy in copies:
        copy.wait()


def pack(k, v, ks, vs):
    rows, wide = k.shape
    return pl.pallas_call(
        pack_kernel,
        out_shape=jax.ShapeDtypeStruct((2 * rows + 2 * SECOND, wide), k.dtype),
        in_specs=[ANY] * 4,
        out_specs=VMEM,
        scratch_shapes=[pltpu.SemaphoreType.DMA((4,))],
        compiler_params=SMALL,
        name="pack",
    )(k, v, ks, vs)


def join_kernel(own_ref, twin_ref, near_ref, far_ref):
    short = far_ref.shape[0] // 2
    for ref in (near_ref, far_ref):
        ref[0:short] = own_ref[0:short]
        ref[short : 2 * short] = twin_ref[0:short]
    near_ref[2 * short :] = twin_ref[short:]


def join(own, twin):
    tall, wide = own.shape
    short = tall - 2 * SECOND
    return pl.pallas_call(
        join_kernel,
        out_shape=(
            jax.ShapeDtypeStruct((tall + short, wide), own.dtype),
            jax.ShapeDtypeStruct((2 * short, wide), own.dtype),
        ),
        in_specs=[VMEM] * 2,
        out_specs=(VMEM, VMEM),
        compiler_params=SMALL,
        name="join",
    )(own, twin)


def lane_token(lane):
    few = WIDTH // SECOND
    return few * (lane // WIDTH) + lane % few, (lane % WIDTH) // few


def masks_kernel(where_ref, pick_ref, near_bias_ref, far_bias_ref, near_extra_ref, far_extra_ref):
    shard = where_ref[0]
    rows = pick_ref.shape[1] // SECOND
    shape = pick_ref.shape
    feature = lax.broadcasted_iota(jnp.int32, shape, 0)
    token, offset = lane_token(lax.broadcasted_iota(jnp.int32, shape, 1))
    pick_ref[...] = (feature == token + offset + 1).astype(jnp.bfloat16)
    early = (shard == 0) & (token + offset < SECOND - 1)
    last = jnp.where(feature == rows, 1.0, jnp.where((feature == rows + 1) & early, NEG, 0.0))
    for ref, hidden in ((near_bias_ref, feature > token), (far_bias_ref, feature <= token)):
        ref[...] = jnp.where((feature < rows) & hidden, NEG, last).astype(jnp.bfloat16)
    for ref, first, cut in (
        (near_extra_ref, shard + 1 - near_extra_ref.shape[0] // rows, near_extra_ref.shape[0] - rows),
        (far_extra_ref, shard - FIRST // rows, 0),
    ):
        row = lax.broadcasted_iota(jnp.int32, ref.shape, 0)
        col = lax.broadcasted_iota(jnp.int32, ref.shape, 1)
        gone = jnp.where(first + row // rows < 0, NEG, 0.0)
        extra = jnp.where(col == rows, gone, jnp.where(col == rows + 1, 1.0, 0.0))
        ref[...] = jnp.where((col < rows) & (row - cut == col), 1.0, extra).astype(jnp.bfloat16)


def masks(where, rows):
    lanes = SECOND * rows
    return pl.pallas_call(
        masks_kernel,
        out_shape=(
            *[jax.ShapeDtypeStruct((HEAD, lanes), jnp.bfloat16)] * 3,
            jax.ShapeDtypeStruct((NEAR * rows, HEAD), jnp.bfloat16),
            jax.ShapeDtypeStruct((FIRST + rows - NEAR * rows, HEAD), jnp.bfloat16),
        ),
        in_specs=[SMEM],
        out_specs=(VMEM,) * 5,
        compiler_params=GRANT,
        name="masks",
    )(where)


def turn_kernel(q_hbm, qt_ref, q, sem):
    copy = pltpu.make_async_copy(q_hbm, q, sem)
    copy.start()
    copy.wait()
    scale = LOG2E / math.sqrt(HEAD)
    few = WIDTH // SECOND
    for h in range(qt_ref.shape[0]):
        part = q[:, h * HEAD : (h + 1) * HEAD].astype(jnp.float32) * scale
        for c in range(qt_ref.shape[1]):
            qt_ref[h, c] = jnp.concatenate([part[c * few : (c + 1) * few]] * (128 // few), axis=0).T


def turn(q):
    rows, wide = q.shape
    heads, chunks = wide // HEAD, SECOND * rows // WIDTH
    return pl.pallas_call(
        turn_kernel,
        out_shape=jax.ShapeDtypeStruct((heads, chunks, HEAD, 128), jnp.float32),
        in_specs=[ANY],
        out_specs=VMEM,
        scratch_shapes=[pltpu.VMEM(q.shape, q.dtype), pltpu.SemaphoreType.DMA(())],
        compiler_params=GRANT,
        name="turn",
    )(q)


def windows(where_ref, ks, vs, x1, y, pick, ksw, svw, rows):
    shard, core = where_ref[0], where_ref[1]
    for own, out, at in ((ks, ksw, 0), (vs, svw, SECOND)):
        near = y[4 * rows + at : 4 * rows + at + SECOND, :]
        twin = x1[2 * rows + at : 2 * rows + at + SECOND, :]
        mine = own[...].astype(jnp.float32)
        tail = jnp.where(core == 1, twin.astype(jnp.float32), near.astype(jnp.float32))
        tail = jnp.where(shard == 0, jnp.zeros_like(tail), tail)
        rest = jnp.zeros((128 - SECOND - rows, mine.shape[1]), jnp.float32)
        tokens = jnp.concatenate([tail, mine, rest], axis=0)
        for g in range(out.shape[0]):
            turned = tokens[:, g * HEAD : (g + 1) * HEAD].T.astype(jnp.bfloat16)
            out[g] = jnp.dot(turned, pick[...], preferred_element_type=jnp.float32)


def stage(kcat, vbuf, vt, extra, start, span):
    window = pl.ds(pl.multiple_of(start, 16), span)
    for g in range(kcat.shape[0]):
        kcat[g, window, HEAD : 2 * HEAD] = extra[...]
        vt[g] = vbuf[window, g * HEAD : (g + 1) * HEAD].T


def run_heads(kcat, start, qt, ksw, svw, bias, vt, sbuf, wbuf, tops, grows, out, peak, norm, before=None):
    kv_heads = ksw.shape[0]
    heads, chunks = qt.shape[:2]
    group = heads // kv_heads
    steps = group * chunks
    window = pl.ds(pl.multiple_of(start, 16), vt.shape[2])
    tiles = [slice(i * 128, (i + 1) * 128) for i in range(WIDTH // 128)]

    def place(step, g):
        step = jnp.minimum(step, steps - 1)
        c = step // group
        return g * group + step % group, c, pl.ds(pl.multiple_of(c * WIDTH, WIDTH), WIDTH)

    def score(step, turn):
        for g in range(kv_heads):
            h, c, at = place(step, g)
            products = jnp.concatenate([qt[h, c]] * len(tiles), axis=1) * ksw[g, :, at]
            products = jnp.concatenate([products.astype(jnp.bfloat16), bias[:, at]], axis=0)
            s = jnp.dot(kcat[g, window, :], products, preferred_element_type=jnp.float32)
            sbuf[turn][g][...] = s
            top = jnp.max(s, axis=0, keepdims=True)
            tops[turn][g][...] = functools.reduce(jnp.maximum, [top[:, t] for t in tiles])

    def soften(step, turn):
        for g in range(kv_heads):
            h, c, _ = place(step, g)
            top = tops[turn][g][...]
            if before is not None:
                top = jnp.maximum(top, before[1][c, pl.ds(h, 1), :])
                grow = jnp.exp2(before[1][c, pl.ds(h, 1), :] - top)
                grows[turn][g][...] = grow
            e = jnp.exp2(sbuf[turn][g][...] - jnp.concatenate([top] * len(tiles), axis=1))
            wbuf[turn][g][...] = e.astype(jnp.bfloat16)
            total = jnp.sum(e, axis=0, keepdims=True)
            total = functools.reduce(jnp.add, [total[:, t] for t in tiles])
            if before is not None:
                total = total + before[2][c, pl.ds(h, 1), :] * grow
            peak[c, pl.ds(h, 1), :] = top
            norm[c, pl.ds(h, 1), :] = total

    def mix(step, turn):
        for g in range(kv_heads):
            h, c, at = place(step, g)
            mixed = jnp.dot(vt[g], wbuf[turn][g][...], preferred_element_type=jnp.float32)
            mixed = mixed * svw[g, :, at]
            sums = functools.reduce(jnp.add, [mixed[:, t] for t in tiles])
            if before is not None:
                sums = sums + before[0][h, c] * grows[turn][g][...]
            out[h, c] = sums

    def several(i, _):
        for turn in range(UNROLL):
            step = UNROLL * i + turn
            mix(step, turn % 2)
            soften(step + 1, (turn + 1) % 2)
            score(step + 2, turn % 2)
        return 0

    score(0, 0)
    score(1, 1)
    soften(0, 0)
    lax.fori_loop(0, steps // UNROLL, several, 0)


def start_all(pairs, sem):
    copies = [pltpu.make_async_copy(a, b, sem.at[i]) for i, (a, b) in enumerate(pairs)]
    for copy in copies:
        copy.start()
    return copies


def block_copies(ref, row, rows, block, kcat, vbuf):
    at = pl.ds(pl.multiple_of(block * rows, rows), rows)
    keys = ref.at[pl.ds(row, rows)]
    pairs = [(keys.at[:, pl.ds(g * HEAD, HEAD)], kcat.at[g, at, pl.ds(0, HEAD)]) for g in range(kcat.shape[0])]
    return pairs + [(ref.at[pl.ds(row + rows, rows)], vbuf.at[at])]


def chip_blocks(ref, rows, pair, flip, kcat, vbuf):
    pairs = []
    for slot in range(2):
        block = 2 * pair + jnp.where(flip == 1, 1 - slot, slot)
        pairs += block_copies(ref, slot * 2 * rows, rows, block, kcat, vbuf)
    return pairs


def near_kernel(
    where_ref, x0_hbm, ks_hbm, vs_hbm, x1_hbm, y_hbm, yp_hbm, qt, pick, bias, extra,
    out_ref, peak_ref, norm_ref, ksw, svw,
    ks, vs, x1, y, kcat, vbuf, vt, sbuf, wbuf, tops, grows, sem,
):
    core = where_ref[1]
    rows = ks.shape[0]
    blocks = vbuf.shape[0] // rows
    pairs = [(ks_hbm, ks), (vs_hbm, vs), (x1_hbm, x1), (y_hbm, y)]
    pairs += block_copies(x0_hbm, 0, rows, blocks - 2 + core, kcat, vbuf)
    pairs += block_copies(x1_hbm, 0, rows, blocks - 1 - core, kcat, vbuf)
    pairs += chip_blocks(y_hbm, rows, 1 - core, core, kcat, vbuf)
    pairs += chip_blocks(yp_hbm, rows, core, 1 - core, kcat, vbuf)
    for copy in start_all(pairs, sem):
        copy.wait()
    windows(where_ref, ks, vs, x1, y, pick, ksw, svw, rows)
    stage(kcat, vbuf, vt, extra, core * rows, NEAR * rows)
    run_heads(kcat, core * rows, qt, ksw, svw, bias, vt, sbuf, wbuf, tops, grows, out_ref, peak_ref, norm_ref)


def far_kernel(
    where_ref, y_hbm, z_hbm, zp_hbm, acc1_ref, peak1_ref, norm1_ref, ksw, svw, qt, bias, extra, w_hbm,
    other_ref, att,
    kcat, vbuf, vt, sbuf, wbuf, tops, grows, out, peak, norm, weight, partial, sem, wsem,
):
    core, side = where_ref[1], where_ref[2]
    rows = att.shape[0]
    half = w_hbm.shape[1] // 2
    blocks = vbuf.shape[0] // rows
    pairs = chip_blocks(z_hbm, rows, core, core, kcat, vbuf)
    pairs += chip_blocks(zp_hbm, rows, 1 - core, 1 - core, kcat, vbuf)
    pairs += block_copies(y_hbm, 2 * rows, rows, blocks - 1, kcat, vbuf)
    copies = start_all(pairs, sem)
    cols = pl.ds(pl.multiple_of((1 - side) * half, 128), half)
    fetch = pltpu.make_async_copy(w_hbm.at[:, cols], weight, wsem)
    fetch.start()
    for copy in copies:
        copy.wait()
    stage(kcat, vbuf, vt, extra, core * rows, (blocks - 1) * rows)
    run_heads(
        kcat, core * rows, qt, ksw, svw, bias, vt, sbuf, wbuf, tops, grows, out, peak, norm, (acc1_ref, peak1_ref, norm1_ref)
    )
    heads, chunks = qt.shape[:2]
    few = WIDTH // SECOND
    shifts = [few << i for i in range((128 // few).bit_length() - 1)]
    factors = []
    for c in range(chunks):
        top = peak[c]
        most = top
        for shift in shifts:
            most = jnp.maximum(most, pltpu.roll(most, shift, 1))
        grow = jnp.exp2(top - most)
        total = norm[c] * grow
        for shift in shifts:
            total = total + pltpu.roll(total, shift, 1)
        factors.append(grow / total)
    fetch.wait()
    for k in range(heads // PAIR):
        for h in range(k * PAIR, (k + 1) * PAIR):
            for c in range(chunks):
                part = (out[h, c] * factors[c][h : h + 1]).T
                part = functools.reduce(jnp.add, [part[i : i + few] for i in range(0, 128, few)])
                att[c * few : (c + 1) * few, h * HEAD : (h + 1) * HEAD] = part.astype(jnp.bfloat16)
        at = slice(k * PAIR * HEAD, (k + 1) * PAIR * HEAD)
        more = jnp.dot(att[:, at], weight[at, :], preferred_element_type=jnp.float32)
        if k == 0:
            partial[...] = more
        elif k < heads // PAIR - 1:
            partial[...] += more
        else:
            other_ref[...] = (partial[...] + more).astype(jnp.bfloat16)


def own_kernel(where_ref, att, w_hbm, mine_ref, weight, sem):
    half = w_hbm.shape[1] // 2
    cols = pl.ds(pl.multiple_of(where_ref[2] * half, 128), half)
    fetch = pltpu.make_async_copy(w_hbm.at[:, cols], weight, sem)
    fetch.start()
    fetch.wait()
    mine_ref[...] = jnp.dot(att[...], weight[...], preferred_element_type=jnp.float32)


def common_scratch(rows, kv_heads, blocks, span):
    def twice(shape, dtype):
        return [[pltpu.VMEM(shape, dtype)] * kv_heads] * 2

    return [
        pltpu.VMEM((kv_heads, blocks * rows, 2 * HEAD), jnp.bfloat16),
        pltpu.VMEM((blocks * rows, kv_heads * HEAD), jnp.bfloat16),
        pltpu.VMEM((kv_heads, HEAD, span), jnp.bfloat16),
        twice((span, WIDTH), jnp.float32),
        twice((span, WIDTH), jnp.bfloat16),
        twice((1, 128), jnp.float32),
        twice((1, 128), jnp.float32),
    ]


def sums_like(qt):
    heads, chunks = qt.shape[:2]
    return [
        jax.ShapeDtypeStruct((heads, chunks, HEAD, 128), jnp.float32),
        *[jax.ShapeDtypeStruct((chunks, heads, 128), jnp.float32)] * 2,
    ]


def attend_near(where, x0, ks, vs, x1, y, yp, qt, pick, bias, extra):
    rows, lanes = ks.shape[0], pick.shape[1]
    kv_heads = ks.shape[1] // HEAD
    return pl.pallas_call(
        near_kernel,
        out_shape=(*sums_like(qt), *[jax.ShapeDtypeStruct((kv_heads, HEAD, lanes), jnp.float32)] * 2),
        in_specs=[SMEM] + [ANY] * 6 + [VMEM] * 4,
        out_specs=(VMEM,) * 5,
        scratch_shapes=[pltpu.VMEM(a.shape, a.dtype) for a in (ks, vs, x1, y)]
        + common_scratch(rows, kv_heads, NEAR + 1, NEAR * rows)
        + [pltpu.SemaphoreType.DMA((22,))],
        compiler_params=GRANT,
        name="near",
    )(where, x0, ks, vs, x1, y, yp, qt, pick, bias, extra)


def attend_far(where, y, z, zp, acc1, peak1, norm1, ksw, svw, qt, bias, extra, w):
    kv_heads, (heads, chunks) = ksw.shape[0], qt.shape[:2]
    rows = ksw.shape[2] // SECOND
    depth, features = w.shape
    span = extra.shape[0]
    return pl.pallas_call(
        far_kernel,
        out_shape=(
            jax.ShapeDtypeStruct((rows, features // 2), jnp.bfloat16),
            jax.ShapeDtypeStruct((rows, heads * HEAD), jnp.bfloat16),
        ),
        in_specs=[SMEM] + [ANY] * 3 + [VMEM] * 8 + [ANY],
        out_specs=(VMEM, VMEM),
        scratch_shapes=common_scratch(rows, kv_heads, span // rows + 1, span)
        + [
            *(pltpu.VMEM(a.shape, a.dtype) for a in (acc1, peak1, norm1)),
            pltpu.VMEM((depth, features // 2), jnp.bfloat16),
            pltpu.VMEM((rows, features // 2), jnp.float32),
            pltpu.SemaphoreType.DMA((15,)),
            pltpu.SemaphoreType.DMA(()),
        ],
        compiler_params=GRANT,
        name="far",
    )(where, y, z, zp, acc1, peak1, norm1, ksw, svw, qt, bias, extra, w)


def project_own(where, att, w):
    rows, (depth, features) = att.shape[0], w.shape
    return pl.pallas_call(
        own_kernel,
        out_shape=jax.ShapeDtypeStruct((rows, features // 2), jnp.float32),
        in_specs=[SMEM, VMEM, ANY],
        out_specs=VMEM,
        scratch_shapes=[pltpu.VMEM((depth, features // 2), jnp.bfloat16), pltpu.SemaphoreType.DMA(())],
        compiler_params=GRANT,
        name="own",
    )(where, att, w)


def body(queries, keys_first, primary_value_array, keys_second, secondary_value_array, out_weight):
    count = lax.axis_size("ctx")
    queries, keys_first, primary_value_array, keys_second, secondary_value_array, out_weight = (
        pltpu.with_memory_space_constraint(a, pltpu.HBM)
        for a in (queries, keys_first, primary_value_array, keys_second, secondary_value_array, out_weight)
    )
    shard = lax.axis_index("ctx")
    where = jnp.stack([shard, shard % 2, lax.axis_index("head")]).astype(jnp.int32)
    packed = pack(keys_first, primary_value_array, keys_second, secondary_value_array)
    twin = core_swap(packed, count)
    near_load, far_load = join(packed, twin)
    near = chip_shift(near_load, count, 1, 2)
    far = chip_shift(far_load, count, 4, 3)
    pick, near_bias, far_bias, near_extra, far_extra = masks(where, queries.shape[0])
    qt = turn(queries)
    near_twin = core_swap(near, count)
    sums = attend_near(
        where, packed, keys_second, secondary_value_array, twin, near, near_twin, qt, pick, near_bias, near_extra
    )
    far_twin = core_swap(far, count)
    other, attention = attend_far(where, near, far, far_twin, *sums, qt, far_bias, far_extra, out_weight)
    other = head_swap(other)
    mine = project_own(where, attention, out_weight)
    return (mine + other.astype(jnp.float32)).astype(jnp.bfloat16)


def solution(mesh):
    in_specs = (P("ctx", "head"),) * 5 + (P("head", None),)
    return jax.shard_map(body, mesh=mesh, in_specs=in_specs, out_specs=P("ctx", "head"), check_vma=False)
```
